32 devices in a mesh: row: 8 (over y, x, core), col: 4 (over z).
Axes of the slice: x: 2, y: 2, z: 4, core: 2. Of those that a mesh axis runs over, the one named last changes fastest.
Arguments:
- documents: float32 [6144, 768], P('row', 'col'), may hold values from -6 to 6
- projection: float32 [768, 768], P('col'), may hold values from -0.21875 to 0.21875
- landmarks: float32 [16384, 768], P('col', 'row'), may hold values from -6 to 6
- coefficients: float32 [16384, 128], P('col'), may hold values from -6 to 6
- inverse_tiles: float32 [16384, 16384], P('col', 'row'), may hold values from -0.046875 to 0.046875
- labels: int32 [6144, 128], P('row'), may hold values 0 or 1
Outputs:
- new_coefficients: float32 [16384, 128], P('col')
- residual: float32 [6144, 128], P('row')
The draws below stay inside these ranges and needn't reach their ends.
All inputs are finite; a program needn't handle non-finite values. No bound on the sum of `labels` on one device may be relied on, other than what follows from the above.
Results may differ from the reference program's by a relative error of at most 0.0001.
Values sent between devices are 32-bit elements; how exact they have to be, the bound alone decides.
A program may use at most 128 MiB of HBM per device.

```python
import jax
import jax.numpy as jnp
from jax import lax

D = 768
M = 16384
LABELS = 128
ITERS = 2
DOCS = 6144


def plant(array, key, smallest, largest):
    spot = [jax.random.randint(jax.random.fold_in(key, axis), (), 0, length) for axis, length in enumerate(array.shape)]
    main_axis = array.shape.index(max(array.shape))
    next_to = spot[:main_axis] + [(spot[main_axis] + 1) % array.shape[main_axis]] + spot[main_axis + 1:]
    return array.at[tuple(spot)].set(smallest).at[tuple(next_to)].set(largest)


def block_levels(key, shape, cuts, low, high):
    level, own = 1.0, jax.random.fold_in(key, 6)
    for axis_at, blocks in cuts:
        draws = jnp.exp(jax.random.uniform(jax.random.fold_in(own, axis_at), (blocks,), jnp.float32, low / len(cuts), high / len(cuts)))
        level = level * jnp.repeat(draws, shape[axis_at] // blocks).reshape([-1 if axis == axis_at else 1 for axis in range(len(shape))])
    return level


def normal_values(own_key, extent, width, bound, split=(), held_as=jnp.bfloat16):
    result = width * jax.random.normal(own_key, extent, jnp.float32)
    if split:
        result = result * block_levels(own_key, extent, split, -0.22, 0.18)
    return jnp.clip(result, -bound, bound).astype(held_as)


def setup_inputs(seed: int = 0) -> dict:
    key_of = jax.random.split(jax.random.key(seed), 7)
    return {
        "documents": normal_values(key_of[0], (DOCS, D), 1.0, 6.0, ((0, 8), (1, 4)), jnp.float32),
        "projection": normal_values(key_of[1], (D, D), D ** -0.5, 0.21875, ((0, 4),), jnp.float32),
        "landmarks": normal_values(key_of[2], (M, D), 1.0, 6.0, ((0, 4), (1, 8)), jnp.float32),
        "coefficients": normal_values(key_of[3], (M, LABELS), 1.0, 6.0, ((0, 4),), jnp.float32),
        "inverse_tiles": normal_values(key_of[4], (M, M), M ** -0.5, 0.046875, ((0, 4), (1, 8)), jnp.float32),
        "labels": plant((jax.random.randint(key_of[5], (DOCS, LABELS), 0, 3) < 1).astype(jnp.int32), jax.random.fold_in(key_of[5], 1), 0, 1),
    }


def reference(documents, projection, landmarks, coefficients, inverse_tiles, labels):
    highest = lax.Precision.HIGHEST
    proj = jnp.dot(documents, projection, precision=highest, preferred_element_type=jnp.float32)
    sq_doc = jnp.sum(proj * proj, axis=1)
    sq_land = jnp.sum(landmarks * landmarks, axis=1)
    inner = jnp.dot(proj, landmarks.T, precision=highest, preferred_element_type=jnp.float32)
    kernel = jnp.exp(-2.0 * (sq_doc[:, None] + sq_land[None, :] - 2.0 * inner) / D)
    step_size = 64.0 / DOCS
    current = coefficients
    target = labels.astype(jnp.float32)
    residual = jnp.zeros((DOCS, LABELS), jnp.float32)
    for iteration in range(ITERS):
        predicted = jnp.dot(kernel, current, precision=highest, preferred_element_type=jnp.float32)
        residual = jax.nn.sigmoid(predicted) - target
        gradient = jnp.dot(kernel.T, residual, precision=highest, preferred_element_type=jnp.float32)
        current = current - step_size * jnp.dot(inverse_tiles, gradient, precision=highest, preferred_element_type=jnp.float32)
    return current, residual
```

```python
import functools

import jax
import jax.numpy as jnp
from jax import lax
from jax.experimental import pallas as pl
from jax.experimental.pallas import tpu as pltpu
from jax.sharding import PartitionSpec as P

ITERS = 2
MESH = pl.DeviceIdType.MESH
VMEM = pl.BlockSpec(memory_space=pltpu.VMEM)
HBM = pl.BlockSpec(memory_space=pl.ANY)


def bit_of(me, bit):
    return lax.rem(lax.div(me, 1 << bit), 2)


def flip(me, bits):
    for bit in bits:
        me = me + (1 << bit) * (1 - 2 * bit_of(me, bit))
    return me


def enter(axes):
    barrier = pltpu.get_barrier_semaphore()
    count = 0
    for axis in axes:
        size = lax.axis_size(axis)
        me = lax.axis_index(axis)
        for other in range(1, size):
            pl.semaphore_signal(
                barrier, inc=1, device_id={axis: lax.rem(me + other, size)}, device_id_type=MESH
            )
        count += size - 1
    pl.semaphore_wait(barrier, count)


def remote(src, dst, send_sem, recv_sem, axis, target):
    return pltpu.make_async_remote_copy(
        src_ref=src,
        dst_ref=dst,
        send_sem=send_sem,
        recv_sem=recv_sem,
        device_id={axis: target},
        device_id_type=MESH,
    )


def held_bits(order, index):
    return [order[i] for i in range(len(order)) if index >> i & 1]


def gather_kernel(
    land, docs, proj, land_out, doc_out, proj_out,
    own_sem, land_send, land_recv, sib_send, sib_recv,
    doc_send, doc_recv, proj_send, proj_recv, psib_send, psib_recv,
):
    rows, cols = lax.axis_size("row"), lax.axis_size("col")
    me, z = lax.axis_index("row"), lax.axis_index("col")
    bits = rows.bit_length() - 1
    shards = rows // 2
    half = land.shape[1] // 2
    phalf = proj.shape[0] // 2
    upper = list(range(bits - 1, 0, -1))
    orders = [upper, upper[1:] + upper[:1]]
    sibling = flip(me, [0])
    enter(("row", "col"))

    locals_ = [
        pltpu.make_async_copy(land, land_out.at[me], own_sem.at[0]),
        pltpu.make_async_copy(docs, doc_out.at[z], own_sem.at[1]),
        pltpu.make_async_copy(proj, proj_out.at[z], own_sem.at[2]),
    ]
    sends = []

    def part(h):
        return pl.ds(h * half, half)

    def slot(h, j):
        return land_out.at[flip(me, held_bits(orders[h], j)), :, part(h)]

    def land_copy(h, j, stage):
        dst = j + (1 << stage)
        return remote(
            land.at[:, part(h)] if j == 0 else slot(h, j),
            slot(h, j),
            land_send.at[h, dst],
            land_recv.at[h, dst],
            "row",
            flip(me, [orders[h][stage]]),
        )

    def sib_copy(h, j):
        return remote(
            land.at[:, part(h)] if j == 0 else slot(h, j),
            slot(h, j), sib_send.at[h, j], sib_recv.at[h, j], "row", sibling,
        )

    def start(copy):
        copy.start()
        sends.append(copy)

    ph = pl.ds(pl.multiple_of(lax.rem(me, 2) * phalf, 8), phalf)
    ph_other = pl.ds(pl.multiple_of(lax.rem(me + 1, 2) * phalf, 8), phalf)

    def chain(d, t):
        sign = 1 - 2 * d
        origin = z - sign * t
        target = z + sign
        valid = (origin >= 0) & (origin < cols) & (target >= 0) & (target < cols)
        doc_src = docs if t == 0 else doc_out.at[origin]
        proj_src = proj.at[ph] if t == 0 else proj_out.at[origin, ph]
        return valid, (
            remote(doc_src, doc_out.at[origin], doc_send.at[d, t], doc_recv.at[d, t], "col", target),
            remote(proj_src, proj_out.at[origin, ph], proj_send.at[d, t], proj_recv.at[d, t], "col", target),
        )

    def arriving(d, t):
        sign = 1 - 2 * d
        origin = z - sign * (t + 1)
        valid = (origin >= 0) & (origin < cols)
        copies = (
            remote(doc_out.at[origin], doc_out.at[origin], doc_send.at[d, t], doc_recv.at[d, t], "col", z),
            remote(proj_out.at[origin, ph], proj_out.at[origin, ph], proj_send.at[d, t], proj_recv.at[d, t], "col", z),
        )
        share = remote(
            proj_out.at[origin, ph], proj_out.at[origin, ph],
            psib_send.at[d, t], psib_recv.at[d, t], "row", sibling,
        )
        incoming = remote(
            proj_out.at[origin, ph_other], proj_out.at[origin, ph_other],
            psib_send.at[d, t], psib_recv.at[d, t], "row", sibling,
        )
        return valid, copies, share, incoming

    for d in range(2):
        valid, copies = chain(d, 0)

        @pl.when(valid)
        def _():
            for copy in copies:
                copy.start()

    for stage in range(bits - 1):
        for h in range(2):
            start(land_copy(h, 0, stage))
    for h in range(2):
        start(sib_copy(h, 0))
    for copy in locals_:
        copy.start()

    def chain_step(t):
        for d in range(2):
            valid, copies, share, _ = arriving(d, t)

            @pl.when(valid)
            def _():
                for copy in copies:
                    copy.wait_recv()
                share.start()

            if t + 1 < cols - 1:
                onward, later = chain(d, t + 1)

                @pl.when(onward)
                def _():
                    for copy in later:
                        copy.start()

    def land_step(j):
        stage = j.bit_length() - 1
        for h in range(2):
            remote(slot(h, j), slot(h, j), land_send.at[h, j], land_recv.at[h, j], "row", me).wait_recv()
            for later in range(stage + 1, bits - 1):
                start(land_copy(h, j, later))
            start(sib_copy(h, j))

    for step in range(max(cols - 1, shards - 1)):
        if step < cols - 1:
            chain_step(step)
        if step + 1 < shards:
            land_step(step + 1)

    for h in range(2):
        for j in range(shards):
            dst = land_out.at[flip(me, [0] + held_bits(orders[h], j)), :, part(h)]
            remote(dst, dst, sib_send.at[h, j], sib_recv.at[h, j], "row", sibling).wait_recv()
    for copy in sends:
        copy.wait_send()
    for copy in locals_:
        copy.wait()
    for d in range(2):
        for t in range(cols - 1):
            valid, copies = chain(d, t)

            @pl.when(valid)
            def _():
                for copy in copies:
                    copy.wait_send()

            came, _, share, incoming = arriving(d, t)

            @pl.when(came)
            def _():
                incoming.wait_recv()
                share.wait_send()


def gather(rows, cols, land, docs, proj):
    shards = rows // 2
    dma = pltpu.SemaphoreType.DMA
    return pl.pallas_call(
        gather_kernel,
        out_shape=(
            jax.ShapeDtypeStruct((rows, *land.shape), land.dtype),
            jax.ShapeDtypeStruct((cols, *docs.shape), docs.dtype),
            jax.ShapeDtypeStruct((cols, *proj.shape), proj.dtype),
        ),
        in_specs=[VMEM] * 3,
        out_specs=(HBM,) * 3,
        scratch_shapes=[dma((3,))] + [dma((2, shards))] * 4 + [dma((2, cols - 1))] * 6,
        compiler_params=pltpu.CompilerParams(collective_id=0, has_side_effects=True),
        name="gather",
    )(land, docs, proj)


def section_orders(count, sections):
    bits = count.bit_length() - 1
    upper = list(range(1, bits))
    return [[0] + upper[h % max(len(upper), 1):] + upper[: h % max(len(upper), 1)] for h in range(sections)]


def group_count(length, blocks, most):
    return max(1, min(most, length // (blocks * 8)))


def waves(groups, stages, finish, begin):
    for wave in range(stages + groups):
        for group in range(groups):
            stage = wave - group
            if 0 <= stage - 1 < stages:
                finish(group, stage - 1)
            if 0 <= stage < stages:
                begin(group, stage)


class Halving:
    def __init__(self, axis, orders, size, bases, src, held, came, send_sem, recv_sem):
        self.axis, self.orders, self.size, self.bases, self.src = axis, orders, size, bases, src
        self.held, self.came, self.send_sem, self.recv_sem = held, came, send_sem, recv_sem
        self.me = lax.axis_index(axis)
        self.starts = [0 for _ in bases]
        self.pending, self.sent = {}, []

    def begin(self, n, stage):
        order = self.orders[n]
        length = self.size >> (stage + 1)
        mine = bit_of(self.me, order[stage])
        base = self.bases[n] if stage == 0 else 0
        keep = pl.ds(pl.multiple_of(base + mine * length, 8), length)
        give = pl.ds(pl.multiple_of(base + (1 - mine) * length, 8), length)
        copy = remote(
            self.src.at[give] if stage == 0 else self.held[stage - 1].at[n, give],
            self.came[stage].at[n], self.send_sem.at[n, stage], self.recv_sem.at[n, stage],
            self.axis, flip(self.me, [order[stage]]),
        )
        copy.start()
        self.starts[n] = self.starts[n] + mine * length
        self.pending[n] = (copy, keep)
        self.sent.append(copy)

    def finish(self, n, stage):
        copy, keep = self.pending[n]
        copy.wait_recv()
        old = self.src[keep, :] if stage == 0 else self.held[stage - 1][n, keep, :]
        self.held[stage][n] = old + self.came[stage][n]

    def end(self):
        for copy in self.sent:
            copy.wait_send()


def stage_scratch(sections, stages, size, width):
    shapes = [pltpu.VMEM((sections, size >> (stage + 1), width), jnp.float32) for stage in range(stages)]
    return shapes + shapes


def all_reduce(axis, orders, size, groups, apply, prepare, src, out, held, came, sems):
    stages = len(orders[0])
    per_group = len(orders) // groups
    me = lax.axis_index(axis)
    bases = [n * size for n in range(len(orders))]
    sums = Halving(axis, orders, size, bases, src, held, came, sems[0], sems[1])
    block = size >> stages
    pending, sent = {}, []

    def members(group):
        return range(group * per_group, (group + 1) * per_group)

    def finish(group, stage):
        for n in members(group):
            if stage < stages:
                sums.finish(n, stage)
                if stage == stages - 1:
                    rows = pl.ds(pl.multiple_of(bases[n] + sums.starts[n], 8), block)
                    out[rows, :] = apply(held[-1][n], rows)
            else:
                back = 2 * stages - 1 - stage
                pending[n].wait_recv()
                sums.starts[n] = sums.starts[n] - bit_of(me, orders[n][back]) * (size >> (back + 1))

    def begin(group, stage):
        for n in members(group):
            if stage < stages:
                if stage == 0:
                    prepare(n)
                sums.begin(n, stage)
            else:
                back = 2 * stages - 1 - stage
                rows = pl.ds(pl.multiple_of(bases[n] + sums.starts[n], 8), size >> (back + 1))
                copy = remote(
                    out.at[rows], out.at[rows], sems[2].at[n, back], sems[3].at[n, back],
                    axis, flip(me, [orders[n][back]]),
                )
                copy.start()
                pending[n] = copy
                sent.append(copy)

    waves(groups, 2 * stages, finish, begin)
    sums.end()
    for copy in sent:
        copy.wait_send()


def gradient_exchange(orders, size, groups, prepare, grad, out, held, came, parts, sems):
    stages = len(orders[0])
    halves = len(orders)
    send_sem, recv_sem, line_send, line_recv, deal_send, deal_recv, own_sem = sems
    rows, cols = lax.axis_size("row"), lax.axis_size("col")
    me, z = lax.axis_index("row"), lax.axis_index("col")
    bases = [(h * groups + g) * size for g in range(groups) for h in range(halves)]
    sums = Halving("row", orders * groups, size, bases, grad, held, came, send_sem, recv_sem)
    length = size >> stages

    def line(g, d, t):
        sign = 1 - 2 * d
        origin = z - sign * t
        target = z + sign
        valid = (origin >= 0) & (origin < cols) & (target >= 0) & (target < cols)
        return valid, remote(
            parts.at[g, origin], parts.at[g, origin], line_send.at[g, d, t], line_recv.at[g, d, t], "col", target
        )

    def came_from(d, t):
        origin = z - (1 - 2 * d) * (t + 1)
        return (origin >= 0) & (origin < cols), origin

    def deal(g, origin, index, first):
        for h in range(halves):
            target = origin * halves + h
            place = out.at[pl.ds(pl.multiple_of(g * size + sums.starts[g * halves + h], 8), length)]
            block = parts.at[g, origin, h]

            @pl.when(target != me)
            def _():
                copy = remote(block, place, deal_send.at[g, index, h], deal_recv.at[g, me], "row", target)
                if first:
                    copy.start()
                else:
                    copy.wait_send()

            @pl.when(target == me)
            def _():
                copy = pltpu.make_async_copy(block, place, own_sem.at[g])
                if first:
                    copy.start()
                else:
                    copy.wait()

    def finish(g, stage):
        if stage < stages:
            for h in range(halves):
                sums.finish(g * halves + h, stage)
                if stage == stages - 1:
                    parts[g, z, h] = held[-1][g * halves + h]
            return
        t = stage - stages
        for d in range(2):
            valid, origin = came_from(d, t)

            @pl.when(valid)
            def _():
                remote(
                    parts.at[g, origin], parts.at[g, origin], line_send.at[g, d, t], line_recv.at[g, d, t], "col", z
                ).wait_recv()

            if t + 1 < cols - 1:
                onward, later = line(g, d, t + 1)

                @pl.when(onward)
                def _():
                    later.start()

            @pl.when(valid)
            def _():
                deal(g, origin, 1 + 2 * t + d, True)

    def begin(g, stage):
        if stage < stages:
            for h in range(halves):
                if stage == 0:
                    prepare(bases[g * halves + h])
                sums.begin(g * halves + h, stage)
        elif stage == stages:
            for d in range(2):
                valid, copy = line(g, d, 0)

                @pl.when(valid)
                def _():
                    copy.start()

            deal(g, z, 0, True)

    waves(groups, stages + cols - 1, finish, begin)
    for g in range(groups):
        first = out.at[pl.ds(0, length)]
        for other in range(1, rows):
            source = lax.rem(me + other, rows)
            remote(first, first, deal_send.at[g, 0, 0], deal_recv.at[g, source], "row", source).wait_recv()
    sums.end()
    for g in range(groups):
        deal(g, z, 0, False)
        for t in range(cols - 1):
            for d in range(2):
                valid, copy = line(g, d, t)

                @pl.when(valid)
                def _():
                    copy.wait_send()

                arrived, origin = came_from(d, t)

                @pl.when(arrived)
                def _():
                    deal(g, origin, 1 + 2 * t + d, False)


def split(x):
    high = x.astype(jnp.bfloat16)
    return high, (x - high.astype(jnp.float32)).astype(jnp.bfloat16)


def dot(a, b):
    return jnp.dot(a, b, preferred_element_type=jnp.float32)


def iterate_kernel(
    step_size, plan, k_high_in, k_low_in, tiles, coefficients, pred_in, labels, cur, res,
    k_high, k_low, tile, pred, grad_both, cur_both, res_both, big, grad, parts, *scratch,
):
    orders, size, groups, res_orders, res_size = plan
    halves, stages, res_stages = len(orders), len(orders[0]), len(res_orders[0])
    scratch = list(scratch)

    def take(count):
        return [scratch.pop(0) for _ in range(count)]

    held, came = take(stages), take(stages)
    res_held, res_came = take(res_stages), take(res_stages)
    res_sems, update_sems, grad_sems, load_sem = take(4), take(4), take(7), take(1)[0]
    width = cur.shape[1]
    sections = halves * groups
    row_step = min(256, size)

    loads = [
        pltpu.make_async_copy(k_high_in, k_high, load_sem.at[0]),
        pltpu.make_async_copy(k_low_in, k_low, load_sem.at[1]),
        pltpu.make_async_copy(coefficients, cur, load_sem.at[2]),
    ]

    def tile_load(n):
        part = pl.ds(n * size, size)
        return pltpu.make_async_copy(tiles.at[part], tile.at[part], load_sem.at[3 + n])

    for copy in loads:
        copy.start()
    for n in range(sections):
        tile_load(n).start()
    enter(("row", "col"))
    pred[...] = pred_in[...]

    def store_split(ref, value):
        high, low = split(value)
        ref[:, :width] = high
        ref[:, width:] = low

    def iteration(it, carry):
        def predict(n):
            @pl.when(it > 0)
            def _():
                rows = pl.ds(n * res_size, res_size)
                wide = dot(k_high[rows, :], cur_both[...])
                pred[rows, :] = wide[:, :width] + wide[:, width:] + dot(k_low[rows, :], cur_both[:, :width])

        @pl.when(it > 0)
        def _():
            store_split(cur_both, cur[...])

        def residual(total, rows):
            return jax.nn.sigmoid(total) - labels[rows, :].astype(jnp.float32)

        all_reduce(
            "col", res_orders, res_size, len(res_orders), residual, predict,
            pred, res, res_held, res_came, res_sems,
        )

        @pl.when(it == 0)
        def _():
            for copy in loads:
                copy.wait()

        high, low = split(res[...].T)
        res_both[:width, :] = high
        res_both[width:, :] = low

        def transposed(base):
            part = pl.ds(base, size)
            wide = dot(res_both[...], k_high[:, part])
            total = wide[:width] + wide[width:] + dot(res_both[:width, :], k_low[:, part])
            big[part, :] = total.T

        gradient_exchange(orders, size, groups, transposed, big, grad, held, came, parts, grad_sems)
        store_split(grad_both, grad[...])

        def product(n):
            @pl.when(it == 0)
            def _():
                tile_load(n).wait()

            for start in range(n * size, (n + 1) * size, row_step):
                rows = pl.ds(start, row_step)
                high, low = split(tile[rows, :])
                wide = dot(high, grad_both[...])
                big[rows, :] = wide[:, :width] + wide[:, width:] + dot(low, grad_both[:, :width])

        def step(total, rows):
            return cur[rows, :] - step_size * total

        all_reduce(
            "row", orders * groups, size, groups, step, product, big, cur, held, came, update_sems
        )
        return carry

    lax.fori_loop(0, ITERS, iteration, 0)


def iterate(rows, cols, step_size, k_high, k_low, tiles, coefficients, pred, labels):
    halves = rows // cols
    length, width = coefficients.shape
    docs, depth = pred.shape[0], tiles.shape[1]
    orders = section_orders(rows, halves)
    stages = len(orders[0])
    groups = group_count(length, halves * rows, 4)
    size = length // (halves * groups)
    sections = halves * groups
    res_groups = group_count(docs, cols, 2)
    res_orders = [list(range(cols.bit_length() - 1))] * res_groups
    res_stages = len(res_orders[0])
    res_size = docs // res_groups
    f32, bf16, dma = jnp.float32, jnp.bfloat16, pltpu.SemaphoreType.DMA
    return pl.pallas_call(
        functools.partial(iterate_kernel, step_size, (orders, size, groups, res_orders, res_size)),
        out_shape=(
            jax.ShapeDtypeStruct((length, width), f32),
            jax.ShapeDtypeStruct((docs, width), f32),
        ),
        in_specs=[HBM] * 4 + [VMEM] * 2,
        out_specs=(VMEM, VMEM),
        scratch_shapes=[
            pltpu.VMEM((docs, length), bf16),
            pltpu.VMEM((docs, length), bf16),
            pltpu.VMEM((length, depth), f32),
            pltpu.VMEM((docs, width), f32),
            pltpu.VMEM((depth, 2 * width), bf16),
            pltpu.VMEM((length, 2 * width), bf16),
            pltpu.VMEM((2 * width, docs), bf16),
            pltpu.VMEM((length, width), f32),
            pltpu.VMEM((depth, width), f32),
            pltpu.VMEM((groups, cols, halves, size >> stages, width), f32),
        ]
        + stage_scratch(sections, stages, size, width)
        + stage_scratch(res_groups, res_stages, res_size, width)
        + [dma((res_groups, res_stages))] * 4
        + [dma((sections, stages))] * 4
        + [dma((sections, stages))] * 2
        + [dma((groups, 2, cols - 1))] * 2
        + [dma((groups, 2 * cols - 1, halves)), dma((groups, rows)), dma((groups,))]
        + [dma((3 + sections,))],
        compiler_params=pltpu.CompilerParams(
            collective_id=1, has_side_effects=True, vmem_limit_bytes=67043328
        ),
        name="iterate",
    )(k_high, k_low, tiles, coefficients, pred, labels)


def kernel_kernel(proj, land, current, out_high, out_low, pred, high_ref, low_ref, square_ref):
    features = land.shape[0]

    @pl.when(pl.program_id(0) == 0)
    def _():
        rows = proj[...]
        high_ref[...], low_ref[...] = split(rows)
        square_ref[...] = jnp.sum(rows * rows, axis=1, keepdims=True)
        pred[...] = jnp.zeros_like(pred)

    def dots(a_high, a_low, b_high, b_low):
        return dot(a_high, b_high) + (dot(a_high, b_low) + dot(a_low, b_high))

    points = land[...]
    inner = dots(high_ref[...], low_ref[...], *split(points))
    squares = square_ref[...] + jnp.sum(points * points, axis=0, keepdims=True)
    tile = jnp.exp(-2.0 * (squares - 2.0 * inner) / features)
    tile_high, tile_low = split(tile)
    out_high[...] = tile_high
    out_low[...] = tile_low
    pred[...] += dots(tile_high, tile_low, *split(current[...]))


def kernel_of(proj, land, current):
    rows, features = proj.shape
    length = land.shape[1]
    width = current.shape[1]
    step = min(512, length)
    return pl.pallas_call(
        kernel_kernel,
        grid=(length // step,),
        out_shape=(
            jax.ShapeDtypeStruct((rows, length), jnp.bfloat16),
            jax.ShapeDtypeStruct((rows, length), jnp.bfloat16),
            jax.ShapeDtypeStruct((rows, width), jnp.float32),
        ),
        in_specs=[
            pl.BlockSpec((rows, features), lambda i: (0, 0)),
            pl.BlockSpec((features, step), lambda i: (0, i)),
            pl.BlockSpec((step, width), lambda i: (i, 0)),
        ],
        out_specs=(
            pl.BlockSpec((rows, step), lambda i: (0, i)),
            pl.BlockSpec((rows, step), lambda i: (0, i)),
            pl.BlockSpec((rows, width), lambda i: (0, 0)),
        ),
        scratch_shapes=[
            pltpu.VMEM((rows, features), jnp.bfloat16),
            pltpu.VMEM((rows, features), jnp.bfloat16),
            pltpu.VMEM((rows, 1), jnp.float32),
        ],
        cost_estimate=pl.CostEstimate(
            flops=6 * rows * length * (features + width),
            bytes_accessed=4 * length * (rows + features),
            transcendentals=rows * length,
        ),
        name="kernel",
    )(proj, land, current)


def on_device(documents, projection, landmarks, coefficients, inverse_tiles, labels):
    rows, cols = lax.axis_size("row"), lax.axis_size("col")
    land_t, docs_t, proj_full = gather(rows, cols, landmarks.T, documents.T, projection)
    land_t = land_t.reshape(-1, land_t.shape[2])
    docs_t = docs_t.reshape(-1, docs_t.shape[2])
    proj_full = proj_full.reshape(-1, proj_full.shape[2])
    projected = lax.dot_general(
        docs_t, proj_full, (((0,), (0,)), ((), ())),
        precision=lax.Precision.HIGH, preferred_element_type=jnp.float32,
    )
    k_high, k_low, predicted = kernel_of(projected, land_t, coefficients)
    step_size = 64.0 / (documents.shape[0] * rows)
    return iterate(rows, cols, step_size, k_high, k_low, inverse_tiles, coefficients, predicted, labels)


def solution(mesh):
    in_specs = (
        P("row", "col"),
        P("col", None),
        P("col", "row"),
        P("col", None),
        P("col", "row"),
        P("row", None),
    )
    out_specs = (P("col", None), P("row", None))
    return jax.shard_map(
        on_device, mesh=mesh, in_specs=in_specs, out_specs=out_specs, check_vma=False
    )
```

```python
import functools

import jax
import jax.numpy as jnp
from jax import lax
from jax.experimental import pallas as pl
from jax.experimental.pallas import tpu as pltpu
from jax.sharding import PartitionSpec as P

ITERS = 2
MESH = pl.DeviceIdType.MESH
VMEM = pl.BlockSpec(memory_space=pltpu.VMEM)
HBM = pl.BlockSpec(memory_space=pl.ANY)


def bit_of(me, bit):
    return lax.rem(lax.div(me, 1 << bit), 2)


def flip(me, bits):
    for bit in bits:
        me = me + (1 << bit) * (1 - 2 * bit_of(me, bit))
    return me


def enter(axes):
    barrier = pltpu.get_barrier_semaphore()
    count = 0
    for axis in axes:
        size = lax.axis_size(axis)
        me = lax.axis_index(axis)
        for other in range(1, size):
            pl.semaphore_signal(
                barrier, inc=1, device_id={axis: lax.rem(me + other, size)}, device_id_type=MESH
            )
        count += size - 1
    pl.semaphore_wait(barrier, count)


def remote(src, dst, send_sem, recv_sem, axis, target):
    return pltpu.make_async_remote_copy(
        src_ref=src,
        dst_ref=dst,
        send_sem=send_sem,
        recv_sem=recv_sem,
        device_id={axis: target},
        device_id_type=MESH,
    )


def held_bits(order, index):
    return [order[i] for i in range(len(order)) if index >> i & 1]


def section_orders(count, sections):
    bits = count.bit_length() - 1
    upper = list(range(1, bits))
    return [[0] + upper[h % max(len(upper), 1):] + upper[: h % max(len(upper), 1)] for h in range(sections)]


def group_count(length, blocks, most):
    return max(1, min(most, length // (blocks * 8)))


def waves(groups, stages, finish, begin):
    for wave in range(stages + groups):
        for group in range(groups):
            stage = wave - group
            if 0 <= stage - 1 < stages:
                finish(group, stage - 1)
            if 0 <= stage < stages:
                begin(group, stage)


class Halving:
    def __init__(self, axis, orders, size, bases, src, held, came, send_sem, recv_sem):
        self.axis, self.orders, self.size, self.bases, self.src = axis, orders, size, bases, src
        self.held, self.came, self.send_sem, self.recv_sem = held, came, send_sem, recv_sem
        self.me = lax.axis_index(axis)
        self.starts = [0 for _ in bases]
        self.pending, self.sent = {}, []

    def begin(self, n, stage):
        order = self.orders[n]
        length = self.size >> (stage + 1)
        mine = bit_of(self.me, order[stage])
        base = self.bases[n] if stage == 0 else 0
        keep = pl.ds(pl.multiple_of(base + mine * length, 8), length)
        give = pl.ds(pl.multiple_of(base + (1 - mine) * length, 8), length)
        copy = remote(
            self.src.at[give] if stage == 0 else self.held[stage - 1].at[n, give],
            self.came[stage].at[n], self.send_sem.at[n, stage], self.recv_sem.at[n, stage],
            self.axis, flip(self.me, [order[stage]]),
        )
        copy.start()
        self.starts[n] = self.starts[n] + mine * length
        self.pending[n] = (copy, keep)
        self.sent.append(copy)

    def finish(self, n, stage):
        copy, keep = self.pending[n]
        copy.wait_recv()
        old = self.src[keep, :] if stage == 0 else self.held[stage - 1][n, keep, :]
        self.held[stage][n] = old + self.came[stage][n]

    def end(self):
        for copy in self.sent:
            copy.wait_send()


def stage_scratch(sections, stages, size, width):
    shapes = [pltpu.VMEM((sections, size >> (stage + 1), width), jnp.float32) for stage in range(stages)]
    return shapes + shapes


def all_reduce(axis, orders, size, groups, apply, prepare, src, out, held, came, sems):
    stages = len(orders[0])
    per_group = len(orders) // groups
    me = lax.axis_index(axis)
    bases = [n * size for n in range(len(orders))]
    sums = Halving(axis, orders, size, bases, src, held, came, sems[0], sems[1])
    block = size >> stages
    pending, sent = {}, []

    def members(group):
        return range(group * per_group, (group + 1) * per_group)

    def finish(group, stage):
        for n in members(group):
            if stage < stages:
                sums.finish(n, stage)
                if stage == stages - 1:
                    rows = pl.ds(pl.multiple_of(bases[n] + sums.starts[n], 8), block)
                    out[rows, :] = apply(held[-1][n], rows)
            else:
                back = 2 * stages - 1 - stage
                pending[n].wait_recv()
                sums.starts[n] = sums.starts[n] - bit_of(me, orders[n][back]) * (size >> (back + 1))

    def begin(group, stage):
        for n in members(group):
            if stage < stages:
                if stage == 0:
                    prepare(n)
                sums.begin(n, stage)
            else:
                back = 2 * stages - 1 - stage
                rows = pl.ds(pl.multiple_of(bases[n] + sums.starts[n], 8), size >> (back + 1))
                copy = remote(
                    out.at[rows], out.at[rows], sems[2].at[n, back], sems[3].at[n, back],
                    axis, flip(me, [orders[n][back]]),
                )
                copy.start()
                pending[n] = copy
                sent.append(copy)

    waves(groups, 2 * stages, finish, begin)
    sums.end()
    for copy in sent:
        copy.wait_send()


def gradient_exchange(orders, size, groups, prepare, grad, out, held, came, parts, sems):
    stages = len(orders[0])
    halves = len(orders)
    send_sem, recv_sem, line_send, line_recv, deal_send, deal_recv, own_sem = sems
    rows, cols = lax.axis_size("row"), lax.axis_size("col")
    me, z = lax.axis_index("row"), lax.axis_index("col")
    bases = [(h * groups + g) * size for g in range(groups) for h in range(halves)]
    sums = Halving("row", orders * groups, size, bases, grad, held, came, send_sem, recv_sem)
    length = size >> stages

    def line(g, d, t):
        sign = 1 - 2 * d
        origin = z - sign * t
        target = z + sign
        valid = (origin >= 0) & (origin < cols) & (target >= 0) & (target < cols)
        return valid, remote(
            parts.at[g, origin], parts.at[g, origin], line_send.at[g, d, t], line_recv.at[g, d, t], "col", target
        )

    def came_from(d, t):
        origin = z - (1 - 2 * d) * (t + 1)
        return (origin >= 0) & (origin < cols), origin

    def deal(g, origin, index, first):
        for h in range(halves):
            target = origin * halves + h
            place = out.at[pl.ds(pl.multiple_of(g * size + sums.starts[g * halves + h], 8), length)]
            block = parts.at[g, origin, h]

            @pl.when(target != me)
            def _():
                copy = remote(block, place, deal_send.at[g, index, h], deal_recv.at[g, me], "row", target)
                if first:
                    copy.start()
                else:
                    copy.wait_send()

            @pl.when(target == me)
            def _():
                copy = pltpu.make_async_copy(block, place, own_sem.at[g])
                if first:
                    copy.start()
                else:
                    copy.wait()

    def finish(g, stage):
        if stage < stages:
            for h in range(halves):
                sums.finish(g * halves + h, stage)
                if stage == stages - 1:
                    parts[g, z, h] = held[-1][g * halves + h]
            return
        t = stage - stages
        for d in range(2):
            valid, origin = came_from(d, t)

            @pl.when(valid)
            def _():
                remote(
                    parts.at[g, origin], parts.at[g, origin], line_send.at[g, d, t], line_recv.at[g, d, t], "col", z
                ).wait_recv()

            if t + 1 < cols - 1:
                onward, later = line(g, d, t + 1)

                @pl.when(onward)
                def _():
                    later.start()

            @pl.when(valid)
            def _():
                deal(g, origin, 1 + 2 * t + d, True)

    def begin(g, stage):
        if stage < stages:
            for h in range(halves):
                if stage == 0:
                    prepare(bases[g * halves + h])
                sums.begin(g * halves + h, stage)
        elif stage == stages:
            for d in range(2):
                valid, copy = line(g, d, 0)

                @pl.when(valid)
                def _():
                    copy.start()

            deal(g, z, 0, True)

    waves(groups, stages + cols - 1, finish, begin)
    for g in range(groups):
        first = out.at[pl.ds(0, length)]
        for other in range(1, rows):
            source = lax.rem(me + other, rows)
            remote(first, first, deal_send.at[g, 0, 0], deal_recv.at[g, source], "row", source).wait_recv()
    sums.end()
    for g in range(groups):
        deal(g, z, 0, False)
        for t in range(cols - 1):
            for d in range(2):
                valid, copy = line(g, d, t)

                @pl.when(valid)
                def _():
                    copy.wait_send()

                arrived, origin = came_from(d, t)

                @pl.when(arrived)
                def _():
                    deal(g, origin, 1 + 2 * t + d, False)


def split(x):
    high = x.astype(jnp.bfloat16)
    return high, (x - high.astype(jnp.float32)).astype(jnp.bfloat16)


def dot(a, b):
    return jnp.dot(a, b, preferred_element_type=jnp.float32)


def iterate_kernel(
    step_size, plan, k_high_in, k_low_in, tiles, coefficients, pred_in, labels, cur, res,
    k_high, k_low, tile, pred, grad_both, cur_both, res_both, big, grad, parts, *scratch,
):
    orders, size, groups, res_orders, res_size = plan
    halves, stages, res_stages = len(orders), len(orders[0]), len(res_orders[0])
    scratch = list(scratch)

    def take(count):
        return [scratch.pop(0) for _ in range(count)]

    held, came = take(stages), take(stages)
    res_held, res_came = take(res_stages), take(res_stages)
    res_sems, update_sems, grad_sems, load_sem = take(4), take(4), take(7), take(1)[0]
    width = cur.shape[1]
    sections = halves * groups
    row_step = min(256, size)

    loads = [
        pltpu.make_async_copy(k_high_in, k_high, load_sem.at[0]),
        pltpu.make_async_copy(k_low_in, k_low, load_sem.at[1]),
        pltpu.make_async_copy(coefficients, cur, load_sem.at[2]),
    ]

    def tile_load(n):
        part = pl.ds(n * size, size)
        return pltpu.make_async_copy(tiles.at[part], tile.at[part], load_sem.at[3 + n])

    for copy in loads:
        copy.start()
    for n in range(sections):
        tile_load(n).start()
    enter(("row", "col"))
    pred[...] = pred_in[...]

    def store_split(ref, value):
        high, low = split(value)
        ref[:, :width] = high
        ref[:, width:] = low

    def iteration(it, carry):
        def predict(n):
            @pl.when(it > 0)
            def _():
                rows = pl.ds(n * res_size, res_size)
                wide = dot(k_high[rows, :], cur_both[...])
                pred[rows, :] = wide[:, :width] + wide[:, width:] + dot(k_low[rows, :], cur_both[:, :width])

        @pl.when(it > 0)
        def _():
            store_split(cur_both, cur[...])

        def residual(total, rows):
            return jax.nn.sigmoid(total) - labels[rows, :].astype(jnp.float32)

        all_reduce(
            "col", res_orders, res_size, len(res_orders), residual, predict,
            pred, res, res_held, res_came, res_sems,
        )

        @pl.when(it == 0)
        def _():
            for copy in loads:
                copy.wait()

        high, low = split(res[...].T)
        res_both[:width, :] = high
        res_both[width:, :] = low

        def transposed(base):
            part = pl.ds(base, size)
            wide = dot(res_both[...], k_high[:, part])
            total = wide[:width] + wide[width:] + dot(res_both[:width, :], k_low[:, part])
            big[part, :] = total.T

        gradient_exchange(orders, size, groups, transposed, big, grad, held, came, parts, grad_sems)
        store_split(grad_both, grad[...])

        def product(n):
            @pl.when(it == 0)
            def _():
                tile_load(n).wait()

            for start in range(n * size, (n + 1) * size, row_step):
                rows = pl.ds(start, row_step)
                high, low = split(tile[rows, :])
                wide = dot(high, grad_both[...])
                big[rows, :] = wide[:, :width] + wide[:, width:] + dot(low, grad_both[:, :width])

        def step(total, rows):
            return cur[rows, :] - step_size * total

        all_reduce(
            "row", orders * groups, size, groups, step, product, big, cur, held, came, update_sems
        )
        return carry

    lax.fori_loop(0, ITERS, iteration, 0)


def iterate(rows, cols, step_size, k_high, k_low, tiles, coefficients, pred, labels):
    halves = rows // cols
    length, width = coefficients.shape
    docs, depth = pred.shape[0], tiles.shape[1]
    orders = section_orders(rows, halves)
    stages = len(orders[0])
    groups = group_count(length, halves * rows, 4)
    size = length // (halves * groups)
    sections = halves * groups
    res_groups = group_count(docs, cols, 2)
    res_orders = [list(range(cols.bit_length() - 1))] * res_groups
    res_stages = len(res_orders[0])
    res_size = docs // res_groups
    f32, bf16, dma = jnp.float32, jnp.bfloat16, pltpu.SemaphoreType.DMA
    return pl.pallas_call(
        functools.partial(iterate_kernel, step_size, (orders, size, groups, res_orders, res_size)),
        out_shape=(
            jax.ShapeDtypeStruct((length, width), f32),
            jax.ShapeDtypeStruct((docs, width), f32),
        ),
        in_specs=[HBM] * 4 + [VMEM] * 2,
        out_specs=(VMEM, VMEM),
        scratch_shapes=[
            pltpu.VMEM((docs, length), bf16),
            pltpu.VMEM((docs, length), bf16),
            pltpu.VMEM((length, depth), f32),
            pltpu.VMEM((docs, width), f32),
            pltpu.VMEM((depth, 2 * width), bf16),
            pltpu.VMEM((length, 2 * width), bf16),
            pltpu.VMEM((2 * width, docs), bf16),
            pltpu.VMEM((length, width), f32),
            pltpu.VMEM((depth, width), f32),
            pltpu.VMEM((groups, cols, halves, size >> stages, width), f32),
        ]
        + stage_scratch(sections, stages, size, width)
        + stage_scratch(res_groups, res_stages, res_size, width)
        + [dma((res_groups, res_stages))] * 4
        + [dma((sections, stages))] * 4
        + [dma((sections, stages))] * 2
        + [dma((groups, 2, cols - 1))] * 2
        + [dma((groups, 2 * cols - 1, halves)), dma((groups, rows)), dma((groups,))]
        + [dma((3 + sections,))],
        compiler_params=pltpu.CompilerParams(
            collective_id=1, has_side_effects=True, vmem_limit_bytes=67043328
        ),
        name="iterate",
    )(k_high, k_low, tiles, coefficients, pred, labels)


def embed_kernel(
    plan, land, docs, proj, coefficients, high_out, low_out, pred,
    land_all, docs_all, proj_all, feat_high, feat_low, square, k_high, k_low,
    own_sem, land_send, land_recv, sib_send, sib_recv, doc_send, doc_recv,
    proj_send, proj_recv, deal_send, deal_recv, pair_send, pair_recv, store_sem,
):
    land_chunks, doc_chunks, pieces = plan
    rows, cols = lax.axis_size("row"), lax.axis_size("col")
    me, z = lax.axis_index("row"), lax.axis_index("col")
    bits = rows.bit_length() - 1
    shards, hops = rows // 2, cols - 1
    half = land.shape[1] // 2
    chunk = half // land_chunks
    doc_chunk = docs.shape[1] // doc_chunks
    features = proj.shape[1]
    upper = list(range(bits - 1, 0, -1))
    orders = [upper, upper[1:] + upper[:1]]
    sibling = flip(me, [0])
    enter(("row", "col"))

    locals_ = [
        pltpu.make_async_copy(land, land_all.at[me], own_sem.at[0]),
        pltpu.make_async_copy(docs, docs_all.at[z], own_sem.at[1]),
        pltpu.make_async_copy(proj, proj_all.at[z], own_sem.at[2]),
    ]
    sends = []

    def start(copy):
        copy.start()
        sends.append(copy)

    def part(h, c):
        return pl.ds(h * half + c * chunk, chunk)

    def slot(h, c, j):
        return land_all.at[flip(me, held_bits(orders[h], j)), :, part(h, c)]

    def land_copy(h, c, j, stage):
        dst = j + (1 << stage)
        return remote(
            land.at[:, part(h, c)] if j == 0 else slot(h, c, j),
            slot(h, c, j), land_send.at[h, c, dst], land_recv.at[h, c, dst],
            "row", flip(me, [orders[h][stage]]),
        )

    def sib_copy(h, c, j):
        return remote(
            land.at[:, part(h, c)] if j == 0 else slot(h, c, j),
            slot(h, c, j), sib_send.at[h, c, j], sib_recv.at[h, c, j], "row", sibling,
        )

    def land_own(c):
        for stage in range(bits - 1):
            for h in range(2):
                start(land_copy(h, c, 0, stage))
        for h in range(2):
            start(sib_copy(h, c, 0))

    def land_step(c, j):
        stage = j.bit_length() - 1
        for h in range(2):
            remote(
                slot(h, c, j), slot(h, c, j), land_send.at[h, c, j], land_recv.at[h, c, j], "row", me
            ).wait_recv()
            for later in range(stage + 1, bits - 1):
                start(land_copy(h, c, j, later))
            start(sib_copy(h, c, j))

    def land_rest(c):
        for j in range(2, shards):
            land_step(c, j)

    def land_ready(c):
        for h in range(2):
            for j in range(shards):
                dst = land_all.at[flip(me, [0] + held_bits(orders[h], j)), :, part(h, c)]
                remote(dst, dst, sib_send.at[h, c, j], sib_recv.at[h, c, j], "row", sibling).wait_recv()

    def onward(d, t):
        sign = 1 - 2 * d
        origin = z - sign * t
        target = z + sign
        return (origin >= 0) & (origin < cols) & (target >= 0) & (target < cols), origin, target

    def arrival(d, t):
        origin = z - (1 - 2 * d) * (t + 1)
        return (origin >= 0) & (origin < cols), origin

    def doc_hop(d, c, t):
        valid, origin, target = onward(d, t)
        cut = pl.ds(c * doc_chunk, doc_chunk)
        dst = docs_all.at[origin, :, cut]
        src = docs.at[:, cut] if t == 0 else dst
        return valid, remote(src, dst, doc_send.at[d, c, t], doc_recv.at[d, c, t], "col", target)

    piece_rows = proj.shape[0] // pieces

    def piece_of(device):
        return pl.ds(pl.multiple_of(lax.rem(device, pieces) * piece_rows, 8), piece_rows)

    def proj_hop(d, t):
        valid, origin, target = onward(d, t)
        dst = proj_all.at[origin, piece_of(me)]
        src = proj.at[piece_of(me)] if t == 0 else dst
        return valid, remote(src, dst, proj_send.at[d, t], proj_recv.at[d, t], "col", target)

    def when_start(hop):
        valid, copy = hop

        @pl.when(valid)
        def _():
            copy.start()

    def when_sent(hop):
        valid, copy = hop

        @pl.when(valid)
        def _():
            copy.wait_send()

    def others(u):
        return [bit + 1 for bit in range(bits) if u >> bit & 1]

    spread = max(pieces // 2, 1)

    def deal_copy(d, t, u, origin):
        place = proj_all.at[origin, piece_of(me)]
        return remote(place, place, deal_send.at[d, t, u], deal_recv.at[d, t, u], "row", flip(me, others(u)))

    def dealt(d, t, u, origin):
        source = flip(me, others(u))
        place = proj_all.at[origin, piece_of(source)]
        return remote(place, place, deal_send.at[d, t, u], deal_recv.at[d, t, u], "row", source)

    def pair_copy(d, t, u, origin, source):
        place = proj_all.at[origin, piece_of(flip(source, others(u)))]
        return remote(place, place, pair_send.at[d, t, u], pair_recv.at[d, t, u], "row", sibling)

    def proj_step(t):
        for d in range(2):
            came, origin = arrival(d, t)
            place = proj_all.at[origin, piece_of(me)]

            @pl.when(came)
            def _():
                remote(place, place, proj_send.at[d, t], proj_recv.at[d, t], "col", z).wait_recv()

            if t + 1 < hops:
                when_start(proj_hop(d, t + 1))

            @pl.when(came)
            def _():
                for u in range(1, spread):
                    deal_copy(d, t, u, origin).start()
                pair_copy(d, t, 0, origin, me).start()

    def proj_share(t):
        for d in range(2):
            came, origin = arrival(d, t)

            @pl.when(came)
            def _():
                for u in range(1, spread):
                    dealt(d, t, u, origin).wait_recv()
                    pair_copy(d, t, u, origin, me).start()

    def proj_ready():
        for t in range(hops):
            for d in range(2):
                came, origin = arrival(d, t)

                @pl.when(came)
                def _():
                    for u in range(spread):
                        pair_copy(d, t, u, origin, sibling).wait_recv()

    def doc_step(c, t):
        for d in range(2):
            came, origin = arrival(d, t)
            place = docs_all.at[origin, :, pl.ds(c * doc_chunk, doc_chunk)]

            @pl.when(came)
            def _():
                remote(place, place, doc_send.at[d, c, t], doc_recv.at[d, c, t], "col", z).wait_recv()

            if t + 1 < hops:
                when_start(doc_hop(d, c, t + 1))

    def doc_own(c):
        for d in range(2):
            when_start(doc_hop(d, c, 0))

    def project(c):
        cut = pl.ds(c * doc_chunk, doc_chunk)
        side = docs_all.shape[0] * docs_all.shape[1]
        high, low = split(docs_all[:, :, cut].reshape(side, doc_chunk).T)
        w_high, w_low = split(proj_all[...].reshape(side, features))
        value = dot(high, w_high) + (dot(high, w_low) + dot(low, w_high))
        feat_high[cut, :], feat_low[cut, :] = split(value)
        square[cut, :] = jnp.sum(value * value, axis=1, keepdims=True)
        pred[cut, :] = jnp.zeros((doc_chunk, pred.shape[1]), jnp.float32)

    stores = []

    def block(first, count, c):
        cut = pl.ds(first * doc_chunk, count * doc_chunk)
        width = pred.shape[1]

        def one(h, carry):
            at = pl.ds(pl.multiple_of(h * half + c * chunk, 128), chunk)
            points = land_all[:, :, at].reshape(features, chunk)
            p_high, p_low = split(points)
            inner = dot(feat_high[cut, :], p_high) + (dot(feat_high[cut, :], p_low) + dot(feat_low[cut, :], p_high))
            squares = square[cut, :] + jnp.sum(points * points, axis=0, keepdims=True)
            high, low = split(jnp.exp(-2.0 * (squares - 2.0 * inner) / features))
            k_high[cut, at] = high
            k_low[cut, at] = low
            c_high, c_low = split(coefficients[at, :])
            wide = dot(high, jnp.concatenate([c_high, c_low], axis=1))
            pred[cut, :] += wide[:, :width] + wide[:, width:] + dot(low, c_high)
            return carry

        lax.fori_loop(0, 2, one, 0)
        for h in range(2):
            at = part(h, c)
            for which, (src, dst) in enumerate(((k_high, high_out), (k_low, low_out))):
                copy = pltpu.make_async_copy(src.at[cut, at], dst.at[cut, at], store_sem.at[first, c, h, which])
                copy.start()
                stores.append(copy)

    for d in range(2):
        when_start(proj_hop(d, 0))
    doc_own(0)
    land_own(0)
    for copy in locals_:
        copy.start()

    def landmark_event(c):
        if shards > 1:
            land_step(c, 1)
        if c + 1 < land_chunks:
            land_own(c + 1)

    proj_step(0)
    landmark_event(0)
    for t in range(1, hops):
        proj_step(t)
    land_rest(0)
    for t in range(hops):
        proj_share(t)
    doc_step(0, 0)
    landmark_event(1)
    for t in range(1, hops - 1):
        doc_step(0, t)
    doc_own(1)
    land_rest(1)
    doc_step(0, hops - 1)
    proj_ready()
    for copy in locals_:
        copy.wait()
    project(0)
    landmark_event(2)
    land_ready(0)
    block(0, 1, 0)
    doc_step(1, 0)
    land_ready(1)
    block(0, 1, 1)
    for t in range(1, hops - 1):
        doc_step(1, t)
    land_rest(2)
    landmark_event(3)
    land_ready(2)
    block(0, 1, 2)
    doc_step(1, hops - 1)
    project(1)
    block(1, 1, 0)
    land_rest(3)
    block(1, 1, 1)
    block(1, 1, 2)
    land_ready(3)
    block(0, 2, 3)

    for copy in sends:
        copy.wait_send()
    for copy in stores:
        copy.wait()
    for d in range(2):
        for t in range(hops):
            when_sent(proj_hop(d, t))
            for c in range(doc_chunks):
                when_sent(doc_hop(d, c, t))
            came, origin = arrival(d, t)

            @pl.when(came)
            def _():
                for u in range(spread):
                    if u > 0:
                        deal_copy(d, t, u, origin).wait_send()
                    pair_copy(d, t, u, origin, me).wait_send()


def embed(rows, cols, land, docs, proj, coefficients):
    length, width = coefficients.shape
    count, features = docs.shape[1], proj.shape[1]
    shards, hops = rows // 2, cols - 1
    pieces = rows
    while proj.shape[0] % (8 * pieces):
        pieces //= 2
    land_chunks, doc_chunks = 4, 2
    spread = max(pieces // 2, 1)
    f32, bf16, dma = jnp.float32, jnp.bfloat16, pltpu.SemaphoreType.DMA
    return pl.pallas_call(
        functools.partial(embed_kernel, (land_chunks, doc_chunks, pieces)),
        out_shape=(
            jax.ShapeDtypeStruct((count, length), bf16),
            jax.ShapeDtypeStruct((count, length), bf16),
            jax.ShapeDtypeStruct((count, width), f32),
        ),
        in_specs=[VMEM] * 4,
        out_specs=(HBM, HBM, VMEM),
        scratch_shapes=[
            pltpu.VMEM((rows, *land.shape), f32),
            pltpu.VMEM((cols, *docs.shape), f32),
            pltpu.VMEM((cols, *proj.shape), f32),
            pltpu.VMEM((count, features), bf16),
            pltpu.VMEM((count, features), bf16),
            pltpu.VMEM((count, 1), f32),
            pltpu.VMEM((count, length), bf16),
            pltpu.VMEM((count, length), bf16),
            dma((3,)),
        ]
        + [dma((2, land_chunks, shards))] * 4
        + [dma((2, doc_chunks, hops))] * 2
        + [dma((2, hops))] * 2
        + [dma((2, hops, spread))] * 4
        + [dma((doc_chunks, land_chunks, 2, 2))],
        compiler_params=pltpu.CompilerParams(
            collective_id=0, has_side_effects=True, vmem_limit_bytes=60 * 1024 * 1024
        ),
        name="embed",
    )(land, docs, proj, coefficients)


def on_device(documents, projection, landmarks, coefficients, inverse_tiles, labels):
    rows, cols = lax.axis_size("row"), lax.axis_size("col")
    k_high, k_low, predicted = embed(rows, cols, landmarks.T, documents.T, projection, coefficients)
    step_size = 64.0 / (documents.shape[0] * rows)
    return iterate(rows, cols, step_size, k_high, k_low, inverse_tiles, coefficients, predicted, labels)


def solution(mesh):
    in_specs = (
        P("row", "col"),
        P("col", None),
        P("col", "row"),
        P("col", None),
        P("col", "row"),
        P("row", None),
    )
    out_specs = (P("col", None), P("row", None))
    return jax.shard_map(
        on_device, mesh=mesh, in_specs=in_specs, out_specs=out_specs, check_vma=False
    )
```

```python
import functools

import jax
import jax.numpy as jnp
from jax import lax
from jax.experimental import pallas as pl
from jax.experimental.pallas import tpu as pltpu
from jax.sharding import PartitionSpec as P

ITERS = 2
MESH = pl.DeviceIdType.MESH
VMEM = pl.BlockSpec(memory_space=pltpu.VMEM)
HBM = pl.BlockSpec(memory_space=pl.ANY)


def bit_of(me, bit):
    return lax.rem(lax.div(me, 1 << bit), 2)


def flip(me, bits):
    for bit in bits:
        me = me + (1 << bit) * (1 - 2 * bit_of(me, bit))
    return me


def enter(axes):
    barrier = pltpu.get_barrier_semaphore()
    count = 0
    for axis in axes:
        size = lax.axis_size(axis)
        me = lax.axis_index(axis)
        for other in range(1, size):
            pl.semaphore_signal(
                barrier, inc=1, device_id={axis: lax.rem(me + other, size)}, device_id_type=MESH
            )
        count += size - 1
    pl.semaphore_wait(barrier, count)


def remote(src, dst, send_sem, recv_sem, axis, target):
    return pltpu.make_async_remote_copy(
        src_ref=src,
        dst_ref=dst,
        send_sem=send_sem,
        recv_sem=recv_sem,
        device_id={axis: target},
        device_id_type=MESH,
    )


def held_bits(order, index):
    return [order[i] for i in range(len(order)) if index >> i & 1]


def section_orders(count, sections):
    bits = count.bit_length() - 1
    upper = list(range(1, bits))
    return [[0] + upper[h % max(len(upper), 1):] + upper[: h % max(len(upper), 1)] for h in range(sections)]


def group_count(length, blocks, most):
    return max(1, min(most, length // (blocks * 8)))


def waves(groups, stages, finish, begin):
    for wave in range(stages + groups):
        for group in range(groups):
            stage = wave - group
            if 0 <= stage - 1 < stages:
                finish(group, stage - 1)
            if 0 <= stage < stages:
                begin(group, stage)


class Halving:
    def __init__(self, axis, orders, size, bases, src, held, came, send_sem, recv_sem):
        self.axis, self.orders, self.size, self.bases, self.src = axis, orders, size, bases, src
        self.held, self.came, self.send_sem, self.recv_sem = held, came, send_sem, recv_sem
        self.me = lax.axis_index(axis)
        self.starts = [0 for _ in bases]
        self.pending, self.sent = {}, []

    def begin(self, n, stage):
        order = self.orders[n]
        length = self.size >> (stage + 1)
        mine = bit_of(self.me, order[stage])
        base = self.bases[n] if stage == 0 else 0
        keep = pl.ds(pl.multiple_of(base + mine * length, 8), length)
        give = pl.ds(pl.multiple_of(base + (1 - mine) * length, 8), length)
        copy = remote(
            self.src.at[give] if stage == 0 else self.held[stage - 1].at[n, give],
            self.came[stage].at[n], self.send_sem.at[n, stage], self.recv_sem.at[n, stage],
            self.axis, flip(self.me, [order[stage]]),
        )
        copy.start()
        self.starts[n] = self.starts[n] + mine * length
        self.pending[n] = (copy, keep)
        self.sent.append(copy)

    def finish(self, n, stage):
        copy, keep = self.pending[n]
        copy.wait_recv()
        old = self.src[keep, :] if stage == 0 else self.held[stage - 1][n, keep, :]
        self.held[stage][n] = old + self.came[stage][n]

    def end(self):
        for copy in self.sent:
            copy.wait_send()


def stage_scratch(sections, stages, size, width):
    shapes = [pltpu.VMEM((sections, size >> (stage + 1), width), jnp.float32) for stage in range(stages)]
    return shapes + shapes


def all_reduce(axis, orders, size, groups, apply, prepare, src, out, held, came, sems):
    stages = len(orders[0])
    per_group = len(orders) // groups
    me = lax.axis_index(axis)
    bases = [n * size for n in range(len(orders))]
    sums = Halving(axis, orders, size, bases, src, held, came, sems[0], sems[1])
    block = size >> stages
    pending, sent = {}, []

    def members(group):
        return range(group * per_group, (group + 1) * per_group)

    def finish(group, stage):
        for n in members(group):
            if stage < stages:
                sums.finish(n, stage)
                if stage == stages - 1:
                    rows = pl.ds(pl.multiple_of(bases[n] + sums.starts[n], 8), block)
                    out[rows, :] = apply(held[-1][n], rows)
            else:
                back = 2 * stages - 1 - stage
                pending[n].wait_recv()
                sums.starts[n] = sums.starts[n] - bit_of(me, orders[n][back]) * (size >> (back + 1))

    def begin(group, stage):
        for n in members(group):
            if stage < stages:
                if stage == 0:
                    prepare(n)
                sums.begin(n, stage)
            else:
                back = 2 * stages - 1 - stage
                rows = pl.ds(pl.multiple_of(bases[n] + sums.starts[n], 8), size >> (back + 1))
                copy = remote(
                    out.at[rows], out.at[rows], sems[2].at[n, back], sems[3].at[n, back],
                    axis, flip(me, [orders[n][back]]),
                )
                copy.start()
                pending[n] = copy
                sent.append(copy)

    waves(groups, 2 * stages, finish, begin)
    sums.end()
    for copy in sent:
        copy.wait_send()


def gradient_exchange(orders, size, groups, prepare, grad, out, held, came, parts, sems):
    stages = len(orders[0])
    halves = len(orders)
    send_sem, recv_sem, line_send, line_recv, deal_send, deal_recv, own_sem = sems
    rows, cols = lax.axis_size("row"), lax.axis_size("col")
    me, z = lax.axis_index("row"), lax.axis_index("col")
    bases = [(h * groups + g) * size for g in range(groups) for h in range(halves)]
    sums = Halving("row", orders * groups, size, bases, grad, held, came, send_sem, recv_sem)
    length = size >> stages

    def line(g, d, t):
        sign = 1 - 2 * d
        origin = z - sign * t
        target = z + sign
        valid = (origin >= 0) & (origin < cols) & (target >= 0) & (target < cols)
        return valid, remote(
            parts.at[g, origin], parts.at[g, origin], line_send.at[g, d, t], line_recv.at[g, d, t], "col", target
        )

    def came_from(d, t):
        origin = z - (1 - 2 * d) * (t + 1)
        return (origin >= 0) & (origin < cols), origin

    def deal(g, origin, index, first):
        for h in range(halves):
            target = origin * halves + h
            place = out.at[pl.ds(pl.multiple_of(g * size + sums.starts[g * halves + h], 8), length)]
            block = parts.at[g, origin, h]

            @pl.when(target != me)
            def _():
                copy = remote(block, place, deal_send.at[g, index, h], deal_recv.at[g, me], "row", target)
                if first:
                    copy.start()
                else:
                    copy.wait_send()

            @pl.when(target == me)
            def _():
                copy = pltpu.make_async_copy(block, place, own_sem.at[g])
                if first:
                    copy.start()
                else:
                    copy.wait()

    def finish(g, stage):
        if stage < stages:
            for h in range(halves):
                sums.finish(g * halves + h, stage)
                if stage == stages - 1:
                    parts[g, z, h] = held[-1][g * halves + h]
            return
        t = stage - stages
        for d in range(2):
            valid, origin = came_from(d, t)

            @pl.when(valid)
            def _():
                remote(
                    parts.at[g, origin], parts.at[g, origin], line_send.at[g, d, t], line_recv.at[g, d, t], "col", z
                ).wait_recv()

            if t + 1 < cols - 1:
                onward, later = line(g, d, t + 1)

                @pl.when(onward)
                def _():
                    later.start()

            @pl.when(valid)
            def _():
                deal(g, origin, 1 + 2 * t + d, True)

    def begin(g, stage):
        if stage < stages:
            for h in range(halves):
                if stage == 0:
                    prepare(bases[g * halves + h])
                sums.begin(g * halves + h, stage)
        elif stage == stages:
            for d in range(2):
                valid, copy = line(g, d, 0)

                @pl.when(valid)
                def _():
                    copy.start()

            deal(g, z, 0, True)

    waves(groups, stages + cols - 1, finish, begin)
    for g in range(groups):
        first = out.at[pl.ds(0, length)]
        for other in range(1, rows):
            source = lax.rem(me + other, rows)
            remote(first, first, deal_send.at[g, 0, 0], deal_recv.at[g, source], "row", source).wait_recv()
    sums.end()
    for g in range(groups):
        deal(g, z, 0, False)
        for t in range(cols - 1):
            for d in range(2):
                valid, copy = line(g, d, t)

                @pl.when(valid)
                def _():
                    copy.wait_send()

                arrived, origin = came_from(d, t)

                @pl.when(arrived)
                def _():
                    deal(g, origin, 1 + 2 * t + d, False)


def split(x):
    high = x.astype(jnp.bfloat16)
    return high, (x - high.astype(jnp.float32)).astype(jnp.bfloat16)


def dot(a, b):
    return jnp.dot(a, b, preferred_element_type=jnp.float32)


def iterate_kernel(
    step_size, plan, k_high_in, k_low_in, tiles, coefficients, pred_in, labels, cur, res,
    k_high, k_low, tile, pred, grad_both, cur_both, res_both, big, grad, parts, *scratch,
):
    orders, size, groups, res_orders, res_size = plan
    halves, stages, res_stages = len(orders), len(orders[0]), len(res_orders[0])
    scratch = list(scratch)

    def take(count):
        return [scratch.pop(0) for _ in range(count)]

    held, came = take(stages), take(stages)
    res_held, res_came = take(res_stages), take(res_stages)
    res_sems, update_sems, grad_sems, load_sem = take(4), take(4), take(7), take(1)[0]
    width = cur.shape[1]
    sections = halves * groups
    row_step = min(256, size)

    loads = [
        pltpu.make_async_copy(k_high_in, k_high, load_sem.at[0]),
        pltpu.make_async_copy(k_low_in, k_low, load_sem.at[1]),
        pltpu.make_async_copy(coefficients, cur, load_sem.at[2]),
    ]

    def tile_load(n):
        part = pl.ds(n * size, size)
        return pltpu.make_async_copy(tiles.at[part], tile.at[part], load_sem.at[3 + n])

    for copy in loads:
        copy.start()
    for n in range(sections):
        tile_load(n).start()
    enter(("row", "col"))
    pred[...] = pred_in[...]

    def store_split(ref, value):
        high, low = split(value)
        ref[:, :width] = high
        ref[:, width:] = low

    def iteration(it, carry):
        def predict(n):
            @pl.when(it > 0)
            def _():
                rows = pl.ds(n * res_size, res_size)
                wide = dot(k_high[rows, :], cur_both[...])
                pred[rows, :] = wide[:, :width] + wide[:, width:] + dot(k_low[rows, :], cur_both[:, :width])

        @pl.when(it > 0)
        def _():
            store_split(cur_both, cur[...])

        def residual(total, rows):
            return jax.nn.sigmoid(total) - labels[rows, :].astype(jnp.float32)

        all_reduce(
            "col", res_orders, res_size, len(res_orders), residual, predict,
            pred, res, res_held, res_came, res_sems,
        )

        @pl.when(it == 0)
        def _():
            for copy in loads:
                copy.wait()

        high, low = split(res[...].T)
        res_both[:width, :] = high
        res_both[width:, :] = low

        def transposed(base):
            part = pl.ds(base, size)
            wide = dot(res_both[...], k_high[:, part])
            total = wide[:width] + wide[width:] + dot(res_both[:width, :], k_low[:, part])
            big[part, :] = total.T

        gradient_exchange(orders, size, groups, transposed, big, grad, held, came, parts, grad_sems)
        store_split(grad_both, grad[...])

        def product(n):
            @pl.when(it == 0)
            def _():
                tile_load(n).wait()

            for start in range(n * size, (n + 1) * size, row_step):
                rows = pl.ds(start, row_step)
                high, low = split(tile[rows, :])
                wide = dot(high, grad_both[...])
                big[rows, :] = wide[:, :width] + wide[:, width:] + dot(low, grad_both[:, :width])

        def step(total, rows):
            return cur[rows, :] - step_size * total

        all_reduce(
            "row", orders * groups, size, groups, step, product, big, cur, held, came, update_sems
        )
        return carry

    lax.fori_loop(0, ITERS, iteration, 0)


def iterate(rows, cols, step_size, k_high, k_low, tiles, coefficients, pred, labels):
    halves = rows // cols
    length, width = coefficients.shape
    docs, depth = pred.shape[0], tiles.shape[1]
    orders = section_orders(rows, halves)
    stages = len(orders[0])
    groups = group_count(length, halves * rows, 2)
    size = length // (halves * groups)
    sections = halves * groups
    res_groups = group_count(docs, cols, 2)
    res_orders = [list(range(cols.bit_length() - 1))] * res_groups
    res_stages = len(res_orders[0])
    res_size = docs // res_groups
    f32, bf16, dma = jnp.float32, jnp.bfloat16, pltpu.SemaphoreType.DMA
    return pl.pallas_call(
        functools.partial(iterate_kernel, step_size, (orders, size, groups, res_orders, res_size)),
        out_shape=(
            jax.ShapeDtypeStruct((length, width), f32),
            jax.ShapeDtypeStruct((docs, width), f32),
        ),
        in_specs=[HBM] * 4 + [VMEM] * 2,
        out_specs=(VMEM, VMEM),
        scratch_shapes=[
            pltpu.VMEM((docs, length), bf16),
            pltpu.VMEM((docs, length), bf16),
            pltpu.VMEM((length, depth), f32),
            pltpu.VMEM((docs, width), f32),
            pltpu.VMEM((depth, 2 * width), bf16),
            pltpu.VMEM((length, 2 * width), bf16),
            pltpu.VMEM((2 * width, docs), bf16),
            pltpu.VMEM((length, width), f32),
            pltpu.VMEM((depth, width), f32),
            pltpu.VMEM((groups, cols, halves, size >> stages, width), f32),
        ]
        + stage_scratch(sections, stages, size, width)
        + stage_scratch(res_groups, res_stages, res_size, width)
        + [dma((res_groups, res_stages))] * 4
        + [dma((sections, stages))] * 4
        + [dma((sections, stages))] * 2
        + [dma((groups, 2, cols - 1))] * 2
        + [dma((groups, 2 * cols - 1, halves)), dma((groups, rows)), dma((groups,))]
        + [dma((3 + sections,))],
        compiler_params=pltpu.CompilerParams(
            collective_id=1, has_side_effects=True, vmem_limit_bytes=67043328
        ),
        name="iterate",
    )(k_high, k_low, tiles, coefficients, pred, labels)


def embed_kernel(
    plan, land, docs, proj, coefficients, high_out, low_out, pred,
    land_all, docs_all, proj_all, feat_high, feat_low, square, k_high, k_low,
    own_sem, land_send, land_recv, sib_send, sib_recv, doc_send, doc_recv,
    proj_send, proj_recv, deal_send, deal_recv, pair_send, pair_recv, store_sem,
):
    land_chunks, doc_chunks, pieces = plan
    rows, cols = lax.axis_size("row"), lax.axis_size("col")
    me, z = lax.axis_index("row"), lax.axis_index("col")
    bits = rows.bit_length() - 1
    shards, hops = rows // 2, cols - 1
    half = land.shape[1] // 2
    chunk = half // land_chunks
    doc_chunk = docs.shape[1] // doc_chunks
    features = proj.shape[1]
    upper = list(range(bits - 1, 0, -1))
    orders = [upper, upper[1:] + upper[:1]]
    sibling = flip(me, [0])
    enter(("row", "col"))

    locals_ = [
        pltpu.make_async_copy(land, land_all.at[me], own_sem.at[0]),
        pltpu.make_async_copy(docs, docs_all.at[z], own_sem.at[1]),
        pltpu.make_async_copy(proj, proj_all.at[z], own_sem.at[2]),
    ]
    sends = []

    def start(copy):
        copy.start()
        sends.append(copy)

    def part(h, c):
        return pl.ds(h * half + c * chunk, chunk)

    def slot(h, c, j):
        return land_all.at[flip(me, held_bits(orders[h], j)), :, part(h, c)]

    def land_copy(h, c, j, stage):
        dst = j + (1 << stage)
        return remote(
            land.at[:, part(h, c)] if j == 0 else slot(h, c, j),
            slot(h, c, j), land_send.at[h, c, dst], land_recv.at[h, c, dst],
            "row", flip(me, [orders[h][stage]]),
        )

    def sib_copy(h, c, j):
        return remote(
            land.at[:, part(h, c)] if j == 0 else slot(h, c, j),
            slot(h, c, j), sib_send.at[h, c, j], sib_recv.at[h, c, j], "row", sibling,
        )

    def land_own(c):
        for stage in range(bits - 1):
            for h in range(2):
                start(land_copy(h, c, 0, stage))
        for h in range(2):
            start(sib_copy(h, c, 0))

    def land_step(c, j):
        stage = j.bit_length() - 1
        for h in range(2):
            remote(
                slot(h, c, j), slot(h, c, j), land_send.at[h, c, j], land_recv.at[h, c, j], "row", me
            ).wait_recv()
            for later in range(stage + 1, bits - 1):
                start(land_copy(h, c, j, later))
            start(sib_copy(h, c, j))

    def land_rest(c):
        for j in range(2, shards):
            land_step(c, j)

    def land_ready(c):
        for h in range(2):
            for j in range(shards):
                dst = land_all.at[flip(me, [0] + held_bits(orders[h], j)), :, part(h, c)]
                remote(dst, dst, sib_send.at[h, c, j], sib_recv.at[h, c, j], "row", sibling).wait_recv()

    def onward(d, t, direct):
        sign = 1 - 2 * d
        origin = z if direct else z - sign * t
        target = z + sign * (t + 1) if direct else z + sign
        return (origin >= 0) & (origin < cols) & (target >= 0) & (target < cols), origin, target

    def arrival(d, t):
        origin = z - (1 - 2 * d) * (t + 1)
        return (origin >= 0) & (origin < cols), origin

    def doc_hop(d, c, t):
        direct = t < 2 or c == 0
        valid, origin, target = onward(d, t, direct)
        cut = pl.ds(c * doc_chunk, doc_chunk)
        dst = docs_all.at[origin, :, cut]
        src = docs.at[:, cut] if direct else dst
        return valid, remote(src, dst, doc_send.at[d, c, t], doc_recv.at[d, c, t], "col", target)

    piece_rows = proj.shape[0] // pieces

    def piece_of(device):
        return pl.ds(pl.multiple_of(lax.rem(device, pieces) * piece_rows, 8), piece_rows)

    def proj_hop(d, t):
        valid, origin, target = onward(d, t, True)
        return valid, remote(proj.at[piece_of(me)], proj_all.at[origin, piece_of(me)], proj_send.at[d, t], proj_recv.at[d, t], "col", target)

    def when_start(hop):
        valid, copy = hop

        @pl.when(valid)
        def _():
            copy.start()

    def when_sent(hop):
        valid, copy = hop

        @pl.when(valid)
        def _():
            copy.wait_send()

    def others(u):
        return [bit + 1 for bit in range(bits) if u >> bit & 1]

    spread = max(pieces // 2, 1)

    def deal_copy(d, t, u, origin):
        place = proj_all.at[origin, piece_of(me)]
        return remote(place, place, deal_send.at[d, t, u], deal_recv.at[d, t, u], "row", flip(me, others(u)))

    def dealt(d, t, u, origin):
        source = flip(me, others(u))
        place = proj_all.at[origin, piece_of(source)]
        return remote(place, place, deal_send.at[d, t, u], deal_recv.at[d, t, u], "row", source)

    def pair_copy(d, t, u, origin, source):
        place = proj_all.at[origin, piece_of(flip(source, others(u)))]
        return remote(place, place, pair_send.at[d, t, u], pair_recv.at[d, t, u], "row", sibling)

    def proj_step(t):
        for d in range(2):
            came, origin = arrival(d, t)
            place = proj_all.at[origin, piece_of(me)]

            @pl.when(came)
            def _():
                remote(place, place, proj_send.at[d, t], proj_recv.at[d, t], "col", z).wait_recv()
                for u in range(1, spread):
                    deal_copy(d, t, u, origin).start()
                pair_copy(d, t, 0, origin, me).start()

    def proj_share(t):
        for d in range(2):
            came, origin = arrival(d, t)

            @pl.when(came)
            def _():
                for u in range(1, spread):
                    dealt(d, t, u, origin).wait_recv()
                    pair_copy(d, t, u, origin, me).start()

    def proj_ready():
        for t in range(hops):
            for d in range(2):
                came, origin = arrival(d, t)

                @pl.when(came)
                def _():
                    for u in range(spread):
                        pair_copy(d, t, u, origin, sibling).wait_recv()

    def doc_step(c, t):
        for d in range(2):
            came, origin = arrival(d, t)
            place = docs_all.at[origin, :, pl.ds(c * doc_chunk, doc_chunk)]

            @pl.when(came)
            def _():
                remote(place, place, doc_send.at[d, c, t], doc_recv.at[d, c, t], "col", z).wait_recv()

            if c > 0 and 2 <= t + 1 < hops:
                when_start(doc_hop(d, c, t + 1))

    def doc_own(c):
        for t in reversed(range(hops if c == 0 else min(2, hops))):
            for d in range(2):
                when_start(doc_hop(d, c, t))

    def project(c):
        cut = pl.ds(c * doc_chunk, doc_chunk)
        side = docs_all.shape[0] * docs_all.shape[1]
        high, low = split(docs_all[:, :, cut].reshape(side, doc_chunk).T)
        w_high, w_low = split(proj_all[...].reshape(side, features))
        value = dot(high, w_high) + (dot(high, w_low) + dot(low, w_high))
        feat_high[cut, :], feat_low[cut, :] = split(value)
        square[cut, :] = jnp.sum(value * value, axis=1, keepdims=True)
        pred[cut, :] = jnp.zeros((doc_chunk, pred.shape[1]), jnp.float32)

    stores = []

    def block(first, count, c):
        cut = pl.ds(first * doc_chunk, count * doc_chunk)
        width = pred.shape[1]

        def one(h, carry):
            at = pl.ds(pl.multiple_of(h * half + c * chunk, 128), chunk)
            points = land_all[:, :, at].reshape(features, chunk)
            p_high, p_low = split(points)
            inner = dot(feat_high[cut, :], p_high) + (dot(feat_high[cut, :], p_low) + dot(feat_low[cut, :], p_high))
            squares = square[cut, :] + jnp.sum(points * points, axis=0, keepdims=True)
            high, low = split(jnp.exp(-2.0 * (squares - 2.0 * inner) / features))
            k_high[cut, at] = high
            k_low[cut, at] = low
            c_high, c_low = split(coefficients[at, :])
            wide = dot(high, jnp.concatenate([c_high, c_low], axis=1))
            pred[cut, :] += wide[:, :width] + wide[:, width:] + dot(low, c_high)
            return carry

        lax.fori_loop(0, 2, one, 0)
        for h in range(2):
            at = part(h, c)
            for which, (src, dst) in enumerate(((k_high, high_out), (k_low, low_out))):
                copy = pltpu.make_async_copy(src.at[cut, at], dst.at[cut, at], store_sem.at[first, c, h, which])
                copy.start()
                stores.append(copy)

    for t in reversed(range(hops)):
        for d in range(2):
            when_start(proj_hop(d, t))
    doc_own(0)
    doc_own(1)
    land_own(0)
    for copy in locals_:
        copy.start()

    def landmark_event(c):
        if shards > 1:
            land_step(c, 1)
        if c + 1 < land_chunks:
            land_own(c + 1)

    landmark_event(0)
    for t in range(hops):
        proj_step(t)
    land_rest(0)
    landmark_event(1)
    for t in range(hops):
        proj_share(t)
    for t in range(hops):
        doc_step(0, t)
    land_rest(1)
    proj_ready()
    for copy in locals_:
        copy.wait()
    project(0)
    land_ready(0)
    block(0, 1, 0)
    landmark_event(2)
    land_ready(1)
    block(0, 1, 1)
    for t in range(hops - 1):
        doc_step(1, t)
    land_rest(2)
    landmark_event(3)
    land_ready(2)
    block(0, 1, 2)
    doc_step(1, hops - 1)
    project(1)
    block(1, 1, 0)
    land_rest(3)
    block(1, 1, 1)
    block(1, 1, 2)
    land_ready(3)
    block(0, 2, 3)

    for copy in sends:
        copy.wait_send()
    for copy in stores:
        copy.wait()
    for d in range(2):
        for t in range(hops):
            when_sent(proj_hop(d, t))
            for c in range(doc_chunks):
                when_sent(doc_hop(d, c, t))
            came, origin = arrival(d, t)

            @pl.when(came)
            def _():
                for u in range(spread):
                    if u > 0:
                        deal_copy(d, t, u, origin).wait_send()
                    pair_copy(d, t, u, origin, me).wait_send()


def embed(rows, cols, land, docs, proj, coefficients):
    length, width = coefficients.shape
    count, features = docs.shape[1], proj.shape[1]
    shards, hops = rows // 2, cols - 1
    pieces = rows
    while proj.shape[0] % (8 * pieces):
        pieces //= 2
    land_chunks, doc_chunks = 4, 2
    spread = max(pieces // 2, 1)
    f32, bf16, dma = jnp.float32, jnp.bfloat16, pltpu.SemaphoreType.DMA
    return pl.pallas_call(
        functools.partial(embed_kernel, (land_chunks, doc_chunks, pieces)),
        out_shape=(
            jax.ShapeDtypeStruct((count, length), bf16),
            jax.ShapeDtypeStruct((count, length), bf16),
            jax.ShapeDtypeStruct((count, width), f32),
        ),
        in_specs=[VMEM] * 4,
        out_specs=(HBM, HBM, VMEM),
        scratch_shapes=[
            pltpu.VMEM((rows, *land.shape), f32),
            pltpu.VMEM((cols, *docs.shape), f32),
            pltpu.VMEM((cols, *proj.shape), f32),
            pltpu.VMEM((count, features), bf16),
            pltpu.VMEM((count, features), bf16),
            pltpu.VMEM((count, 1), f32),
            pltpu.VMEM((count, length), bf16),
            pltpu.VMEM((count, length), bf16),
            dma((3,)),
        ]
        + [dma((2, land_chunks, shards))] * 4
        + [dma((2, doc_chunks, hops))] * 2
        + [dma((2, hops))] * 2
        + [dma((2, hops, spread))] * 4
        + [dma((doc_chunks, land_chunks, 2, 2))],
        compiler_params=pltpu.CompilerParams(
            collective_id=0, has_side_effects=True, vmem_limit_bytes=60 * 1024 * 1024
        ),
        name="embed",
    )(land, docs, proj, coefficients)


def on_device(documents, projection, landmarks, coefficients, inverse_tiles, labels):
    rows, cols = lax.axis_size("row"), lax.axis_size("col")
    k_high, k_low, predicted = embed(rows, cols, landmarks.T, documents.T, projection, coefficients)
    step_size = 64.0 / (documents.shape[0] * rows)
    return iterate(rows, cols, step_size, k_high, k_low, inverse_tiles, coefficients, predicted, labels)


def solution(mesh):
    in_specs = (
        P("row", "col"),
        P("col", None),
        P("col", "row"),
        P("col", None),
        P("col", "row"),
        P("row", None),
    )
    out_specs = (P("col", None), P("row", None))
    return jax.shard_map(
        on_device, mesh=mesh, in_specs=in_specs, out_specs=out_specs, check_vma=False
    )
```

```python
import functools

import jax
import jax.numpy as jnp
from jax import lax
from jax.experimental import pallas as pl
from jax.experimental.pallas import tpu as pltpu
from jax.sharding import PartitionSpec as P

ITERS = 2
MESH = pl.DeviceIdType.MESH
VMEM = pl.BlockSpec(memory_space=pltpu.VMEM)
HBM = pl.BlockSpec(memory_space=pl.ANY)


def bit_of(me, bit):
    return lax.rem(lax.div(me, 1 << bit), 2)


def flip(me, bits):
    for bit in bits:
        me = me + (1 << bit) * (1 - 2 * bit_of(me, bit))
    return me


def enter(axes):
    barrier = pltpu.get_barrier_semaphore()
    count = 0
    for axis in axes:
        size = lax.axis_size(axis)
        me = lax.axis_index(axis)
        for other in range(1, size):
            pl.semaphore_signal(
                barrier, inc=1, device_id={axis: lax.rem(me + other, size)}, device_id_type=MESH
            )
        count += size - 1
    pl.semaphore_wait(barrier, count)


def remote(src, dst, send_sem, recv_sem, axis, target):
    return pltpu.make_async_remote_copy(
        src_ref=src,
        dst_ref=dst,
        send_sem=send_sem,
        recv_sem=recv_sem,
        device_id={axis: target},
        device_id_type=MESH,
    )


def held_bits(order, index):
    return [order[i] for i in range(len(order)) if index >> i & 1]


def section_orders(count, sections):
    bits = count.bit_length() - 1
    upper = list(range(1, bits))
    return [[0] + upper[h % max(len(upper), 1):] + upper[: h % max(len(upper), 1)] for h in range(sections)]


def group_count(length, blocks, most):
    return max(1, min(most, length // (blocks * 8)))


def waves(groups, stages, finish, begin):
    for wave in range(stages + groups):
        for group in range(groups):
            stage = wave - group
            if 0 <= stage - 1 < stages:
                finish(group, stage - 1)
            if 0 <= stage < stages:
                begin(group, stage)


class Halving:
    def __init__(self, axis, orders, size, bases, src, held, came, send_sem, recv_sem):
        self.axis, self.orders, self.size, self.bases, self.src = axis, orders, size, bases, src
        self.held, self.came, self.send_sem, self.recv_sem = held, came, send_sem, recv_sem
        self.me = lax.axis_index(axis)
        self.starts = [0 for _ in bases]
        self.pending, self.sent = {}, []

    def begin(self, n, stage):
        order = self.orders[n]
        length = self.size >> (stage + 1)
        mine = bit_of(self.me, order[stage])
        base = self.bases[n] if stage == 0 else 0
        keep = pl.ds(pl.multiple_of(base + mine * length, 8), length)
        give = pl.ds(pl.multiple_of(base + (1 - mine) * length, 8), length)
        copy = remote(
            self.src.at[give] if stage == 0 else self.held[stage - 1].at[n, give],
            self.came[stage].at[n], self.send_sem.at[n, stage], self.recv_sem.at[n, stage],
            self.axis, flip(self.me, [order[stage]]),
        )
        copy.start()
        self.starts[n] = self.starts[n] + mine * length
        self.pending[n] = (copy, keep)
        self.sent.append(copy)

    def finish(self, n, stage):
        copy, keep = self.pending[n]
        copy.wait_recv()
        old = self.src[keep, :] if stage == 0 else self.held[stage - 1][n, keep, :]
        self.held[stage][n] = old + self.came[stage][n]

    def end(self):
        for copy in self.sent:
            copy.wait_send()


def stage_scratch(sections, stages, size, width):
    shapes = [pltpu.VMEM((sections, size >> (stage + 1), width), jnp.float32) for stage in range(stages)]
    return shapes + shapes


def all_reduce(axis, orders, size, groups, apply, prepare, src, out, held, came, sems):
    stages = len(orders[0])
    per_group = len(orders) // groups
    me = lax.axis_index(axis)
    bases = [n * size for n in range(len(orders))]
    sums = Halving(axis, orders, size, bases, src, held, came, sems[0], sems[1])
    block = size >> stages
    pending, sent = {}, []

    def members(group):
        return range(group * per_group, (group + 1) * per_group)

    def finish(group, stage):
        for n in members(group):
            if stage < stages:
                sums.finish(n, stage)
                if stage == stages - 1:
                    rows = pl.ds(pl.multiple_of(bases[n] + sums.starts[n], 8), block)
                    out[rows, :] = apply(held[-1][n], rows)
            else:
                back = 2 * stages - 1 - stage
                pending[n].wait_recv()
                sums.starts[n] = sums.starts[n] - bit_of(me, orders[n][back]) * (size >> (back + 1))

    def begin(group, stage):
        for n in members(group):
            if stage < stages:
                if stage == 0:
                    prepare(n)
                sums.begin(n, stage)
            else:
                back = 2 * stages - 1 - stage
                rows = pl.ds(pl.multiple_of(bases[n] + sums.starts[n], 8), size >> (back + 1))
                copy = remote(
                    out.at[rows], out.at[rows], sems[2].at[n, back], sems[3].at[n, back],
                    axis, flip(me, [orders[n][back]]),
                )
                copy.start()
                pending[n] = copy
                sent.append(copy)

    waves(groups, 2 * stages, finish, begin)
    sums.end()
    for copy in sent:
        copy.wait_send()


def direct_all_reduce(axis, groups, apply, prepare, src, out, came, sems):
    others = came.shape[1]
    size = others + 1
    block = came.shape[2]
    me = lax.axis_index(axis)
    sent = []

    def place(group, owner):
        return pl.ds(pl.multiple_of((group * size + owner) * block, 8), block)

    def send(source, target_ref, group, other, sem):
        copy = remote(
            source, target_ref, sems[sem].at[group, other], sems[sem + 1].at[group, other],
            axis, lax.rem(me + other + 1, size),
        )
        copy.start()
        sent.append(copy)

    for group in range(groups):
        prepare(group)
        for other in range(others):
            owner = lax.rem(me + other + 1, size)
            send(src.at[place(group, owner)], came.at[group, other], group, other, 0)
    arrivals = []
    for group in range(groups):
        mine = place(group, me)
        total = src[mine, :]
        for other in range(others):
            slot = came.at[group, other]
            source = lax.rem(me + size - other - 1, size)
            remote(slot, slot, sems[0].at[group, other], sems[1].at[group, other], axis, source).wait_recv()
            total = total + came[group, other]
        out[mine, :] = apply(total, mine)
        for other in range(others):
            send(out.at[mine], out.at[mine], group, other, 2)
            source = lax.rem(me + size - other - 1, size)
            theirs = out.at[place(group, source)]
            arrivals.append(
                remote(theirs, theirs, sems[2].at[group, other], sems[3].at[group, other], axis, source)
            )
    for copy in arrivals:
        copy.wait_recv()
    for copy in sent:
        copy.wait_send()


def gradient_exchange(orders, size, groups, prepare, grad, out, held, came, parts, sems):
    stages = len(orders[0])
    halves = len(orders)
    send_sem, recv_sem, line_send, line_recv, deal_send, deal_recv, own_sem = sems
    rows, cols = lax.axis_size("row"), lax.axis_size("col")
    me, z = lax.axis_index("row"), lax.axis_index("col")
    bases = [(h * groups + g) * size for g in range(groups) for h in range(halves)]
    sums = Halving("row", orders * groups, size, bases, grad, held, came, send_sem, recv_sem)
    length = size >> stages

    def line(g, d, t):
        sign = 1 - 2 * d
        origin = z - sign * t
        target = z + sign
        valid = (origin >= 0) & (origin < cols) & (target >= 0) & (target < cols)
        return valid, remote(
            parts.at[g, origin], parts.at[g, origin], line_send.at[g, d, t], line_recv.at[g, d, t], "col", target
        )

    def came_from(d, t):
        origin = z - (1 - 2 * d) * (t + 1)
        return (origin >= 0) & (origin < cols), origin

    def deal(g, origin, index, first):
        for h in range(halves):
            target = origin * halves + h
            place = out.at[pl.ds(pl.multiple_of(g * size + sums.starts[g * halves + h], 8), length)]
            block = parts.at[g, origin, h]

            @pl.when(target != me)
            def _():
                copy = remote(block, place, deal_send.at[g, index, h], deal_recv.at[g, me], "row", target)
                if first:
                    copy.start()
                else:
                    copy.wait_send()

            @pl.when(target == me)
            def _():
                copy = pltpu.make_async_copy(block, place, own_sem.at[g])
                if first:
                    copy.start()
                else:
                    copy.wait()

    def finish(g, stage):
        if stage < stages:
            for h in range(halves):
                sums.finish(g * halves + h, stage)
                if stage == stages - 1:
                    parts[g, z, h] = held[-1][g * halves + h]
            return
        t = stage - stages
        for d in range(2):
            valid, origin = came_from(d, t)

            @pl.when(valid)
            def _():
                remote(
                    parts.at[g, origin], parts.at[g, origin], line_send.at[g, d, t], line_recv.at[g, d, t], "col", z
                ).wait_recv()

            if t + 1 < cols - 1:
                onward, later = line(g, d, t + 1)

                @pl.when(onward)
                def _():
                    later.start()

            @pl.when(valid)
            def _():
                deal(g, origin, 1 + 2 * t + d, True)

    def begin(g, stage):
        if stage < stages:
            for h in range(halves):
                if stage == 0:
                    prepare(bases[g * halves + h])
                sums.begin(g * halves + h, stage)
        elif stage == stages:
            for d in range(2):
                valid, copy = line(g, d, 0)

                @pl.when(valid)
                def _():
                    copy.start()

            deal(g, z, 0, True)

    waves(groups, stages + cols - 1, finish, begin)
    for g in range(groups):
        first = out.at[pl.ds(0, length)]
        for other in range(1, rows):
            source = lax.rem(me + other, rows)
            remote(first, first, deal_send.at[g, 0, 0], deal_recv.at[g, source], "row", source).wait_recv()
    sums.end()
    for g in range(groups):
        deal(g, z, 0, False)
        for t in range(cols - 1):
            for d in range(2):
                valid, copy = line(g, d, t)

                @pl.when(valid)
                def _():
                    copy.wait_send()

                arrived, origin = came_from(d, t)

                @pl.when(arrived)
                def _():
                    deal(g, origin, 1 + 2 * t + d, False)


def split(x):
    high = x.astype(jnp.bfloat16)
    return high, (x - high.astype(jnp.float32)).astype(jnp.bfloat16)


def dot(a, b):
    return jnp.dot(a, b, preferred_element_type=jnp.float32)


def iterate_kernel(
    step_size, plan, k_high_in, k_low_in, tiles, coefficients, pred_in, labels, cur, res,
    k_high, k_low, tile, pred, grad_both, cur_both, res_both, big, grad, parts, *scratch,
):
    orders, size, groups, res_groups, res_size = plan
    halves, stages = len(orders), len(orders[0])
    scratch = list(scratch)

    def take(count):
        return [scratch.pop(0) for _ in range(count)]

    held, came = take(stages), take(stages)
    res_came = take(1)[0]
    res_sems, update_sems, grad_sems, load_sem = take(4), take(4), take(7), take(1)[0]
    width = cur.shape[1]
    sections = halves * groups
    row_step = min(256, size)

    loads = [
        pltpu.make_async_copy(k_high_in, k_high, load_sem.at[0]),
        pltpu.make_async_copy(k_low_in, k_low, load_sem.at[1]),
        pltpu.make_async_copy(coefficients, cur, load_sem.at[2]),
    ]

    def tile_load(n):
        part = pl.ds(n * size, size)
        return pltpu.make_async_copy(tiles.at[part], tile.at[part], load_sem.at[3 + n])

    for copy in loads:
        copy.start()
    for n in range(sections):
        tile_load(n).start()
    enter(("row", "col"))
    pred[...] = pred_in[...]

    def store_split(ref, value):
        high, low = split(value)
        ref[:, :width] = high
        ref[:, width:] = low

    def iteration(it, carry):
        def predict(n):
            @pl.when(it > 0)
            def _():
                rows = pl.ds(n * res_size, res_size)
                wide = dot(k_high[rows, :], cur_both[...])
                pred[rows, :] = wide[:, :width] + wide[:, width:] + dot(k_low[rows, :], cur_both[:, :width])

        @pl.when(it > 0)
        def _():
            store_split(cur_both, cur[...])

        def residual(total, rows):
            return jax.nn.sigmoid(total) - labels[rows, :].astype(jnp.float32)

        direct_all_reduce("col", res_groups, residual, predict, pred, res, res_came, res_sems)

        @pl.when(it == 0)
        def _():
            for copy in loads:
                copy.wait()

        high, low = split(res[...].T)
        res_both[:width, :] = high
        res_both[width:, :] = low

        def transposed(base):
            part = pl.ds(base, size)
            wide = dot(res_both[...], k_high[:, part])
            total = wide[:width] + wide[width:] + dot(res_both[:width, :], k_low[:, part])
            big[part, :] = total.T

        gradient_exchange(orders, size, groups, transposed, big, grad, held, came, parts, grad_sems)
        store_split(grad_both, grad[...])

        def product(n):
            @pl.when(it == 0)
            def _():
                tile_load(n).wait()

            for start in range(n * size, (n + 1) * size, row_step):
                rows = pl.ds(start, row_step)
                high, low = split(tile[rows, :])
                wide = dot(high, grad_both[...])
                big[rows, :] = wide[:, :width] + wide[:, width:] + dot(low, grad_both[:, :width])

        def step(total, rows):
            return cur[rows, :] - step_size * total

        all_reduce(
            "row", orders * groups, size, groups, step, product, big, cur, held, came, update_sems
        )
        return carry

    lax.fori_loop(0, ITERS, iteration, 0)


def iterate(rows, cols, step_size, k_high, k_low, tiles, coefficients, pred, labels):
    halves = rows // cols
    length, width = coefficients.shape
    docs, depth = pred.shape[0], tiles.shape[1]
    orders = section_orders(rows, halves)
    stages = len(orders[0])
    groups = group_count(length, halves * rows, 2)
    size = length // (halves * groups)
    sections = halves * groups
    res_groups = group_count(docs, cols, 2)
    res_size = docs // res_groups
    f32, bf16, dma = jnp.float32, jnp.bfloat16, pltpu.SemaphoreType.DMA
    return pl.pallas_call(
        functools.partial(iterate_kernel, step_size, (orders, size, groups, res_groups, res_size)),
        out_shape=(
            jax.ShapeDtypeStruct((length, width), f32),
            jax.ShapeDtypeStruct((docs, width), f32),
        ),
        in_specs=[HBM] * 4 + [VMEM] * 2,
        out_specs=(VMEM, VMEM),
        scratch_shapes=[
            pltpu.VMEM((docs, length), bf16),
            pltpu.VMEM((docs, length), bf16),
            pltpu.VMEM((length, depth), f32),
            pltpu.VMEM((docs, width), f32),
            pltpu.VMEM((depth, 2 * width), bf16),
            pltpu.VMEM((length, 2 * width), bf16),
            pltpu.VMEM((2 * width, docs), bf16),
            pltpu.VMEM((length, width), f32),
            pltpu.VMEM((depth, width), f32),
            pltpu.VMEM((groups, cols, halves, size >> stages, width), f32),
        ]
        + stage_scratch(sections, stages, size, width)
        + [pltpu.VMEM((res_groups, cols - 1, res_size // cols, width), f32)]
        + [dma((res_groups, cols - 1))] * 4
        + [dma((sections, stages))] * 4
        + [dma((sections, stages))] * 2
        + [dma((groups, 2, cols - 1))] * 2
        + [dma((groups, 2 * cols - 1, halves)), dma((groups, rows)), dma((groups,))]
        + [dma((3 + sections,))],
        compiler_params=pltpu.CompilerParams(
            collective_id=1, has_side_effects=True, vmem_limit_bytes=67043328
        ),
        name="iterate",
    )(k_high, k_low, tiles, coefficients, pred, labels)


def embed_kernel(
    plan, land, docs, proj, coefficients, high_out, low_out, pred,
    land_all, docs_all, proj_all, feat_high, feat_low, square, k_high, k_low,
    own_sem, land_send, land_recv, sib_send, sib_recv, doc_send, doc_recv,
    proj_send, proj_recv, deal_send, deal_recv, pair_send, pair_recv, store_sem,
):
    land_chunks, doc_chunks, pieces = plan
    rows, cols = lax.axis_size("row"), lax.axis_size("col")
    me, z = lax.axis_index("row"), lax.axis_index("col")
    bits = rows.bit_length() - 1
    shards, hops = rows // 2, cols - 1
    half = land.shape[1] // 2
    chunk = half // land_chunks
    doc_chunk = docs.shape[1] // doc_chunks
    features = proj.shape[1]
    upper = list(range(bits - 1, 0, -1))
    orders = [upper, upper[1:] + upper[:1]]
    sibling = flip(me, [0])
    enter(("row", "col"))

    locals_ = [
        pltpu.make_async_copy(land, land_all.at[me], own_sem.at[0]),
        pltpu.make_async_copy(docs, docs_all.at[z], own_sem.at[1]),
        pltpu.make_async_copy(proj, proj_all.at[z], own_sem.at[2]),
    ]
    sends = []

    def start(copy):
        copy.start()
        sends.append(copy)

    def part(h, c):
        return pl.ds(h * half + c * chunk, chunk)

    def slot(h, c, j):
        return land_all.at[flip(me, held_bits(orders[h], j)), :, part(h, c)]

    def land_copy(h, c, j, stage):
        dst = j + (1 << stage)
        return remote(
            land.at[:, part(h, c)] if j == 0 else slot(h, c, j),
            slot(h, c, j), land_send.at[h, c, dst], land_recv.at[h, c, dst],
            "row", flip(me, [orders[h][stage]]),
        )

    def sib_copy(h, c, j):
        return remote(
            land.at[:, part(h, c)] if j == 0 else slot(h, c, j),
            slot(h, c, j), sib_send.at[h, c, j], sib_recv.at[h, c, j], "row", sibling,
        )

    def land_own(c):
        for stage in range(bits - 1):
            for h in range(2):
                start(land_copy(h, c, 0, stage))
        for h in range(2):
            start(sib_copy(h, c, 0))

    def land_step(c, j):
        stage = j.bit_length() - 1
        for h in range(2):
            remote(
                slot(h, c, j), slot(h, c, j), land_send.at[h, c, j], land_recv.at[h, c, j], "row", me
            ).wait_recv()
            for later in range(stage + 1, bits - 1):
                start(land_copy(h, c, j, later))
            start(sib_copy(h, c, j))

    def land_rest(c):
        for j in range(2, shards):
            land_step(c, j)

    def land_ready(c):
        for h in range(2):
            for j in range(shards):
                dst = land_all.at[flip(me, [0] + held_bits(orders[h], j)), :, part(h, c)]
                remote(dst, dst, sib_send.at[h, c, j], sib_recv.at[h, c, j], "row", sibling).wait_recv()

    def onward(d, t, direct):
        sign = 1 - 2 * d
        origin = z if direct else z - sign * t
        target = z + sign * (t + 1) if direct else z + sign
        return (origin >= 0) & (origin < cols) & (target >= 0) & (target < cols), origin, target

    def arrival(d, t):
        origin = z - (1 - 2 * d) * (t + 1)
        return (origin >= 0) & (origin < cols), origin

    def doc_hop(d, c, t):
        direct = t < 2
        valid, origin, target = onward(d, t, direct)
        cut = pl.ds(c * doc_chunk, doc_chunk)
        dst = docs_all.at[origin, :, cut]
        src = docs.at[:, cut] if direct else dst
        return valid, remote(src, dst, doc_send.at[d, c, t], doc_recv.at[d, c, t], "col", target)

    piece_rows = proj.shape[0] // pieces

    def piece_of(device):
        return pl.ds(pl.multiple_of(lax.rem(device, pieces) * piece_rows, 8), piece_rows)

    def proj_hop(d, t):
        valid, origin, target = onward(d, t, True)
        return valid, remote(proj.at[piece_of(me)], proj_all.at[origin, piece_of(me)], proj_send.at[d, t], proj_recv.at[d, t], "col", target)

    def when_start(hop):
        valid, copy = hop

        @pl.when(valid)
        def _():
            copy.start()

    def when_sent(hop):
        valid, copy = hop

        @pl.when(valid)
        def _():
            copy.wait_send()

    def others(u):
        return [bit + 1 for bit in range(bits) if u >> bit & 1]

    spread = max(pieces // 2, 1)

    def deal_copy(d, t, u, origin):
        place = proj_all.at[origin, piece_of(me)]
        return remote(place, place, deal_send.at[d, t, u], deal_recv.at[d, t, u], "row", flip(me, others(u)))

    def dealt(d, t, u, origin):
        source = flip(me, others(u))
        place = proj_all.at[origin, piece_of(source)]
        return remote(place, place, deal_send.at[d, t, u], deal_recv.at[d, t, u], "row", source)

    def pair_copy(d, t, u, origin, source):
        place = proj_all.at[origin, piece_of(flip(source, others(u)))]
        return remote(place, place, pair_send.at[d, t, u], pair_recv.at[d, t, u], "row", sibling)

    def proj_step(t):
        for d in range(2):
            came, origin = arrival(d, t)
            place = proj_all.at[origin, piece_of(me)]

            @pl.when(came)
            def _():
                remote(place, place, proj_send.at[d, t], proj_recv.at[d, t], "col", z).wait_recv()
                for u in range(1, spread):
                    deal_copy(d, t, u, origin).start()
                pair_copy(d, t, 0, origin, me).start()

    def proj_share(t):
        for d in range(2):
            came, origin = arrival(d, t)

            @pl.when(came)
            def _():
                for u in range(1, spread):
                    dealt(d, t, u, origin).wait_recv()
                    pair_copy(d, t, u, origin, me).start()

    def proj_ready():
        for t in range(hops):
            for d in range(2):
                came, origin = arrival(d, t)

                @pl.when(came)
                def _():
                    for u in range(spread):
                        pair_copy(d, t, u, origin, sibling).wait_recv()

    def doc_step(c, t):
        for d in range(2):
            came, origin = arrival(d, t)
            place = docs_all.at[origin, :, pl.ds(c * doc_chunk, doc_chunk)]

            @pl.when(came)
            def _():
                remote(place, place, doc_send.at[d, c, t], doc_recv.at[d, c, t], "col", z).wait_recv()

            if 2 <= t + 1 < hops:
                when_start(doc_hop(d, c, t + 1))

    def doc_own(c):
        for t in reversed(range(min(2, hops))):
            for d in range(2):
                when_start(doc_hop(d, c, t))

    def project(c):
        cut = pl.ds(c * doc_chunk, doc_chunk)
        side = docs_all.shape[0] * docs_all.shape[1]
        high, low = split(docs_all[:, :, cut].reshape(side, doc_chunk).T)
        w_high, w_low = split(proj_all[...].reshape(side, features))
        value = dot(high, w_high) + (dot(high, w_low) + dot(low, w_high))
        feat_high[cut, :], feat_low[cut, :] = split(value)
        square[cut, :] = jnp.sum(value * value, axis=1, keepdims=True)
        pred[cut, :] = jnp.zeros((doc_chunk, pred.shape[1]), jnp.float32)

    stores = []

    def block(first, count, c):
        cut = pl.ds(first * doc_chunk, count * doc_chunk)
        width = pred.shape[1]

        def one(h, carry):
            at = pl.ds(pl.multiple_of(h * half + c * chunk, 128), chunk)
            points = land_all[:, :, at].reshape(features, chunk)
            p_high, p_low = split(points)
            inner = dot(feat_high[cut, :], p_high) + (dot(feat_high[cut, :], p_low) + dot(feat_low[cut, :], p_high))
            squares = square[cut, :] + jnp.sum(points * points, axis=0, keepdims=True)
            high, low = split(jnp.exp(-2.0 * (squares - 2.0 * inner) / features))
            k_high[cut, at] = high
            k_low[cut, at] = low
            c_high, c_low = split(coefficients[at, :])
            wide = dot(high, jnp.concatenate([c_high, c_low], axis=1))
            pred[cut, :] += wide[:, :width] + wide[:, width:] + dot(low, c_high)
            return carry

        lax.fori_loop(0, 2, one, 0)
        for h in range(2):
            at = part(h, c)
            for which, (src, dst) in enumerate(((k_high, high_out), (k_low, low_out))):
                copy = pltpu.make_async_copy(src.at[cut, at], dst.at[cut, at], store_sem.at[first, c, h, which])
                copy.start()
                stores.append(copy)

    for t in reversed(range(hops)):
        for d in range(2):
            when_start(proj_hop(d, t))
    doc_own(0)
    land_own(0)
    for copy in locals_:
        copy.start()

    def landmark_event(c):
        if shards > 1:
            land_step(c, 1)
        if c + 1 < land_chunks:
            land_own(c + 1)

    landmark_event(0)
    for t in range(hops):
        proj_step(t)
    land_rest(0)
    landmark_event(1)
    for t in range(1, hops - 1):
        doc_step(0, t)
    doc_own(1)
    for t in range(hops):
        proj_share(t)
    for t in sorted({0, hops - 1}):
        doc_step(0, t)
    land_rest(1)
    proj_ready()
    for copy in locals_:
        copy.wait()
    project(0)
    land_ready(0)
    block(0, 1, 0)
    landmark_event(2)
    for t in range(1, hops - 1):
        doc_step(1, t)
    land_ready(1)
    block(0, 1, 1)
    land_rest(2)
    landmark_event(3)
    land_ready(2)
    block(0, 1, 2)
    for t in sorted({0, hops - 1}):
        doc_step(1, t)
    project(1)
    block(1, 1, 0)
    land_rest(3)
    block(1, 1, 1)
    block(1, 1, 2)
    land_ready(3)
    block(0, 2, 3)

    for copy in sends:
        copy.wait_send()
    for copy in stores:
        copy.wait()
    for d in range(2):
        for t in range(hops):
            when_sent(proj_hop(d, t))
            for c in range(doc_chunks):
                when_sent(doc_hop(d, c, t))
            came, origin = arrival(d, t)

            @pl.when(came)
            def _():
                for u in range(spread):
                    if u > 0:
                        deal_copy(d, t, u, origin).wait_send()
                    pair_copy(d, t, u, origin, me).wait_send()


def embed(rows, cols, land, docs, proj, coefficients):
    length, width = coefficients.shape
    count, features = docs.shape[1], proj.shape[1]
    shards, hops = rows // 2, cols - 1
    pieces = rows
    while proj.shape[0] % (8 * pieces):
        pieces //= 2
    land_chunks, doc_chunks = 4, 2
    spread = max(pieces // 2, 1)
    f32, bf16, dma = jnp.float32, jnp.bfloat16, pltpu.SemaphoreType.DMA
    return pl.pallas_call(
        functools.partial(embed_kernel, (land_chunks, doc_chunks, pieces)),
        out_shape=(
            jax.ShapeDtypeStruct((count, length), bf16),
            jax.ShapeDtypeStruct((count, length), bf16),
            jax.ShapeDtypeStruct((count, width), f32),
        ),
        in_specs=[VMEM] * 4,
        out_specs=(HBM, HBM, VMEM),
        scratch_shapes=[
            pltpu.VMEM((rows, *land.shape), f32),
            pltpu.VMEM((cols, *docs.shape), f32),
            pltpu.VMEM((cols, *proj.shape), f32),
            pltpu.VMEM((count, features), bf16),
            pltpu.VMEM((count, features), bf16),
            pltpu.VMEM((count, 1), f32),
            pltpu.VMEM((count, length), bf16),
            pltpu.VMEM((count, length), bf16),
            dma((3,)),
        ]
        + [dma((2, land_chunks, shards))] * 4
        + [dma((2, doc_chunks, hops))] * 2
        + [dma((2, hops))] * 2
        + [dma((2, hops, spread))] * 4
        + [dma((doc_chunks, land_chunks, 2, 2))],
        compiler_params=pltpu.CompilerParams(
            collective_id=0, has_side_effects=True, vmem_limit_bytes=60 * 1024 * 1024
        ),
        name="embed",
    )(land, docs, proj, coefficients)


def on_device(documents, projection, landmarks, coefficients, inverse_tiles, labels):
    rows, cols = lax.axis_size("row"), lax.axis_size("col")
    k_high, k_low, predicted = embed(rows, cols, landmarks.T, documents.T, projection, coefficients)
    step_size = 64.0 / (documents.shape[0] * rows)
    return iterate(rows, cols, step_size, k_high, k_low, inverse_tiles, coefficients, predicted, labels)


def solution(mesh):
    in_specs = (
        P("row", "col"),
        P("col", None),
        P("col", "row"),
        P("col", None),
        P("col", "row"),
        P("row", None),
    )
    out_specs = (P("col", None), P("row", None))
    return jax.shard_map(
        on_device, mesh=mesh, in_specs=in_specs, out_specs=out_specs, check_vma=False
    )
```
